512 devices in a mesh: grp: 4 (over x_lo, core), dp: 32 (over z, x_hi), mp: 4 (over y).
Axes of the slice: x: 4 (x_hi: 2, x_lo: 2; x = x_hi * 2 + x_lo), y: 4, z: 16, core: 2. Of those that a mesh axis runs over, the one named last changes fastest.
Arguments:
- neighbours: bfloat16 [512, 256, 896], P(('grp', 'dp')), may hold values from -6 to 6
- counts: int32 [512], P(('grp', 'dp')), may hold values from 0 to 2
- owner: int32 [512], P(('grp', 'dp')), may hold values from 0 to 511, as said below
- norm_gain: float32 [896], replicated, may hold values from 0.1 to 1.9
- w_in: bfloat16 [896, 3584], P('dp', 'mp'), may hold values from -0.1875 to 0.1875
- w_out: bfloat16 [3584, 896], P('mp', 'dp'), may hold values from -0.09375 to 0.09375
- w_key: bfloat16 [896, 4096], P('dp', 'mp'), may hold values from -0.1875 to 0.1875
- w_value: bfloat16 [896, 4096], P('dp', 'mp'), may hold values from -0.1875 to 0.1875
- queries: bfloat16 [32768, 4096], P(('grp', 'dp'), 'mp'), may hold values from -150 to 150
Outputs:
- attended: bfloat16 [32768, 4096], P(('grp', 'dp'), 'mp')
The draws below stay inside these ranges and needn't reach their ends.
Inputs may be any that keep to these rules, and one draw needn't show every extreme that they name: owner is a permutation of the 512 query blocks. Span c stands on device c // 4 of grp+dp (index grp * 32 + dp); block owner[c] lies on device owner[c] // 4, which has the same dp index. Each device keeps 2 of its spans (their blocks lie on the device itself) and sends the other 2 to one other device along grp.
All inputs are finite; a program needn't handle non-finite values.
Results may differ from the reference program's by a relative error of at most 0.02.
Values may be sent and summed in bfloat16 or wider, within the bound.
A program may use at most 64 MiB of HBM per device.

```python
import jax
import jax.numpy as jnp
from jax import lax

D = 4096
HEAD = 128
ENC_D = 896
ENC_FF = 3584
SPAN = 64
NLEN = 128
NBR = 2
SP_DEV = 4
SPANS = 512
TOKENS = 32768
N_GRP = 4
N_DP = 32


def draw_owner(key, part):
    half = SP_DEV // 2
    key_tau = jax.random.fold_in(key, 11)
    key_sigma = jax.random.fold_in(key, 12)
    key_offset = jax.random.fold_in(key, 13)
    taus = jax.vmap(lambda k: jax.random.permutation(k, SP_DEV))(jax.random.split(key_tau, N_GRP * N_DP)).reshape(N_GRP, N_DP, SP_DEV)
    sigmas = jax.vmap(lambda k: jax.random.permutation(k, SP_DEV))(jax.random.split(key_sigma, N_GRP * N_DP)).reshape(N_GRP, N_DP, SP_DEV)
    offsets = jax.random.randint(key_offset, (N_DP,), 1, N_GRP)
    grp_index = jnp.arange(N_GRP, dtype=jnp.int32)[:, None, None]
    dp_index = jnp.arange(N_DP, dtype=jnp.int32)[None, :, None]
    local = jnp.arange(SP_DEV, dtype=jnp.int32)[None, None, :]
    target = jnp.where(local < half, grp_index, (grp_index + offsets[None, :, None]) % N_GRP)
    target = jnp.broadcast_to(target, (N_GRP, N_DP, SP_DEV)).astype(jnp.int32)
    dp_full = jnp.broadcast_to(dp_index, (N_GRP, N_DP, SP_DEV))
    local_full = jnp.broadcast_to(local, (N_GRP, N_DP, SP_DEV))
    slot = sigmas[target, dp_full, local_full]
    value = ((target * N_DP + dp_full) * SP_DEV + slot).astype(jnp.int32)
    grp_full = jnp.broadcast_to(grp_index, (N_GRP, N_DP, SP_DEV))
    result = jnp.zeros((N_GRP, N_DP, SP_DEV), jnp.int32).at[grp_full, dp_full, taus].set(value)
    return result.reshape(SPANS)


def draw_queries(key, part):
    base = jax.random.normal(jax.random.fold_in(key, 21), (TOKENS, D), jnp.float32)
    values = jnp.clip(base, -6.0, 6.0)
    return values.astype(jnp.bfloat16)


def touch_ends(values, key, least, high):
    index_at = [jax.random.randint(jax.random.fold_in(key, axis), (), 0, length) for axis, length in enumerate(values.shape)]
    longest = values.shape.index(max(values.shape))
    neighbour = index_at[:longest] + [(index_at[longest] + 1) % values.shape[longest]] + index_at[longest + 1:]
    return values.at[tuple(index_at)].set(least).at[tuple(neighbour)].set(high)


def block_levels(own_key, extent, pieces, low, top_value):
    loudness = 1.0
    for axis_at, shards_of in pieces:
        heights = jax.random.uniform(jax.random.fold_in(jax.random.fold_in(own_key, 6), axis_at), (shards_of,), jnp.float32, low / len(pieces), top_value / len(pieces))
        loudness = loudness * jnp.repeat(jnp.exp(heights), extent[axis_at] // shards_of).reshape((-1,) + (1,) * (len(extent) - 1 - axis_at))
    return loudness


def scatter_about(rng, dims, width, limit, cuts=(), kind=jnp.bfloat16):
    drawn = jax.random.normal(rng, dims, jnp.float32) * width
    if len(cuts) > 0:
        drawn = block_levels(rng, dims, cuts, -0.22, 0.18) * drawn
    return jnp.clip(drawn, min=-limit, max=limit).astype(kind)


def setup_inputs(seed: int = 0) -> dict:
    seeds = jax.random.split(jax.random.key(seed), 10)
    return {
        "neighbours": scatter_about(seeds[0], (SPANS, NBR * NLEN, ENC_D), 1.0, 6.0, ((0, 128),)),
        "counts": touch_ends(jax.random.randint(seeds[1], (SPANS,), 0, 3), jax.random.fold_in(seeds[1], 1), 0, 2).astype(jnp.int32),
        "owner": draw_owner(jax.random.fold_in(seeds[9], 71), 0),
        "norm_gain": jnp.clip(1.0 + 0.18 * jax.random.normal(seeds[3], (ENC_D,), jnp.float32), 0.1, 1.9),
        "w_in": scatter_about(seeds[4], (ENC_D, ENC_FF), ENC_D ** -0.5, 0.1875, ((0, 32), (1, 4))),
        "w_out": scatter_about(seeds[5], (ENC_FF, ENC_D), ENC_FF ** -0.5, 0.09375, ((0, 4), (1, 32))),
        "w_key": scatter_about(seeds[6], (ENC_D, D), ENC_D ** -0.5, 0.1875, ((0, 32), (1, 4))),
        "w_value": scatter_about(seeds[7], (ENC_D, D), ENC_D ** -0.5, 0.1875, ((0, 32), (1, 4))),
        "queries": draw_queries(jax.random.fold_in(seeds[9], 71), 0),
    }


def encode(block, norm_gain, w_in, w_out):
    count = block.shape[0]
    flat = block.astype(jnp.float32).reshape(-1, ENC_D)
    meansq = lax.optimization_barrier(jnp.mean(flat * flat, axis=-1, keepdims=True))
    normed = (flat * lax.rsqrt(meansq + 1e-06) * norm_gain).astype(jnp.bfloat16)
    pre = jnp.dot(normed, w_in, preferred_element_type=jnp.float32)
    hidden = jax.nn.gelu(pre, approximate=False).astype(jnp.bfloat16)
    total = jnp.dot(hidden, w_out, preferred_element_type=jnp.float32)
    return (flat + total).astype(jnp.bfloat16).reshape(count, NBR * NLEN, ENC_D)

def attend(query_block, states, live_counts, w_key, w_value):
    count = states.shape[0]
    flat = states.reshape(-1, ENC_D)
    heads = w_key.shape[1] // HEAD
    keys = jnp.dot(flat, w_key, preferred_element_type=jnp.float32).astype(jnp.bfloat16)
    values = jnp.dot(flat, w_value, preferred_element_type=jnp.float32).astype(jnp.bfloat16)
    keys = keys.reshape(count, NBR * NLEN, heads, HEAD).astype(jnp.float32)
    values = values.reshape(count, NBR * NLEN, heads, HEAD).astype(jnp.float32)
    qfull = query_block.reshape(count, SPAN, heads, HEAD).astype(jnp.float32)
    scores = jnp.einsum('cqhd,ckhd->chqk', qfull, keys) * HEAD ** (-0.5)
    position = jnp.arange(NBR * NLEN, dtype=jnp.int32) // NLEN
    live = (position[None, :] < live_counts[:, None])[:, None, None, :]
    masked = jnp.where(live, scores, -1e+30)
    top = jnp.maximum(lax.optimization_barrier(jnp.max(masked, axis=-1)), 0.0)
    probs = jnp.where(live, jnp.exp(masked - top[..., None]), 0.0)
    denom = lax.optimization_barrier(jnp.sum(probs, axis=-1)) + jnp.exp(-top)
    weights = probs.astype(jnp.bfloat16).astype(jnp.float32)
    mixed = jnp.einsum('chqk,ckhd->cqhd', weights, values)
    mixed = mixed / jnp.transpose(denom, (0, 2, 1))[..., None]
    return mixed.astype(jnp.bfloat16).reshape(count, SPAN, heads * HEAD)

def reference(neighbours, counts, owner, norm_gain, w_in, w_out, w_key, w_value, queries):
    inverse = jnp.zeros((SPANS,), jnp.int32).at[owner].set(jnp.arange(SPANS, dtype=jnp.int32))
    query_blocks = queries.reshape(SPANS, SPAN, D)

    def one_block(slots):
        source = inverse[slots]
        states = encode(neighbours[source], norm_gain, w_in, w_out)
        return attend(query_blocks[slots], states, counts[source], w_key, w_value)
    result = lax.map(one_block, jnp.arange(SPANS, dtype=jnp.int32).reshape(-1, SP_DEV))
    return result.reshape(TOKENS, D)
```

```python
import functools

import jax
import jax.numpy as jnp
from jax import lax
from jax.experimental import pallas as pl
from jax.experimental.pallas import tpu as pltpu
from jax.sharding import PartitionSpec as P

HEAD = 128
NLEN = 128
MESH = pl.DeviceIdType.MESH
HALF = 16


def ring_place():
    g, d, m = (lax.axis_index(name) for name in ("grp", "dp", "mp"))
    core, x, z = g % 2, (d % 2) * 2 + g // 2, d // 2
    return core, x, z, m


def chip_core(x, core, z, m):
    return ((x % 2) * 2 + core, z * 2 + x // 2, m)


class Gather:
    def __init__(self, zs, own_ref, out_ref, sems):
        self.zs, self.out = zs, out_ref
        (self.zsend, self.zrecv, self.fsend, self.frecv, self.one, self.psend, self.precv) = sems
        self.core, self.x, self.z, self.m = ring_place()
        turn = 1 - 2 * self.core
        self.xf, self.xb = (self.x + 4 + turn) % 4, (self.x + 4 - turn) % 4
        self.xo = (self.x + 2) % 4
        self.own = own_ref.at[self.x % 2, self.core]

    def partners(self):
        z, zs = self.z, self.zs
        return [
            chip_core(self.x, self.core, (z + 1) % zs, self.m),
            chip_core(self.x, self.core, (z + zs - 1) % zs, self.m),
            chip_core(self.xf, self.core, z, self.m),
            chip_core(self.xb, self.core, z, self.m),
            chip_core(self.x, 1 - self.core, z, self.m),
        ]

    def copy(self, src, dst, send, recv, to):
        return pltpu.make_async_remote_copy(
            src_ref=src, dst_ref=dst, send_sem=send, recv_sem=recv, device_id=to, device_id_type=MESH
        )

    def slot(self, x, z):
        return self.out.at[x, self.core, z]

    def piece(self, x):
        return self.out.at[x, self.core]

    def ring(self, plus, s):
        zs = self.zs
        at = (self.z + zs - s) % zs if plus else (self.z + s) % zs
        to = self.partners()[0 if plus else 1]
        src = self.own if s == 0 else self.slot(self.x, at)
        row = 0 if plus else 1
        return self.copy(src, self.slot(self.x, at), self.zsend.at[row, s], self.zrecv.at[row, s], to)

    def arrived(self, plus, s):
        zs = self.zs
        at = (self.z + zs - s) % zs if plus else (self.z + s) % zs
        row = 0 if plus else 1
        ref = self.slot(self.x, at)
        self.copy(ref, ref, self.zsend.at[row, s - 1], self.zrecv.at[row, s - 1], self.partners()[0]).wait_recv()

    def across(self, at, j, own):
        src = self.own if own else self.slot(self.x, at)
        dst = self.slot(self.x, at)
        to = self.partners()
        self.copy(src, dst, self.fsend, self.frecv.at[j], to[2]).start()
        self.copy(src, dst, self.one.at[0], self.one.at[1], to[3]).start()

    def relay(self, at, j):
        ref = self.slot(self.xb, at)
        self.copy(ref, ref, self.fsend, self.frecv.at[j], self.partners()[2]).wait_recv()
        self.copy(ref, ref, self.one.at[2], self.one.at[3], self.partners()[2]).start()

    def fresh(self, s):
        zs = self.zs
        if s == 0:
            return [(self.z, 0)]
        found = [((self.z + zs - s) % zs, 2 * s - 1)]
        if s <= (zs - 1) // 2:
            found.append(((self.z + s) % zs, 2 * s))
        return found

    def run(self, local):
        last, back = self.zs // 2, (self.zs - 1) // 2
        keep = pltpu.make_async_copy(self.own, self.slot(self.x, self.z), local)
        keep.start()
        for s in range(last + 1):
            if s > 0:
                self.arrived(True, s)
            if s < last:
                self.ring(True, s).start()
            if 0 < s <= back:
                self.arrived(False, s)
            if s < back:
                self.ring(False, s).start()
            for at, j in self.fresh(s):
                self.across(at, j, s == 0)
            if s > 0:
                for at, j in self.fresh(s - 1):
                    self.relay(at, j)
        keep.wait()
        to = self.partners()[4]
        swaps = []

        def swap(x):
            ref = self.piece(x)
            i = len(swaps)
            swaps.append(self.copy(ref, ref, self.psend.at[i], self.precv.at[i], to))
            swaps[-1].start()

        swap(self.x)
        for at, j in self.fresh(last):
            self.relay(at, j)
        swap(self.xb)
        whole = self.piece(self.xf)
        self.copy(whole, whole, self.one.at[0], self.one.at[1], to).wait_recv()
        swap(self.xf)
        whole = self.piece(self.xo)
        self.copy(whole, whole, self.one.at[2], self.one.at[3], to).wait_recv()
        swap(self.xo)
        for s in range(last):
            self.ring(True, s).wait_send()
            if s < back:
                self.ring(False, s).wait_send()
        whole = self.piece(self.x)
        for sem in (self.fsend, self.one.at[0], self.one.at[2]):
            self.copy(whole, whole, sem, self.one.at[1], to).wait_send()
        for i, x in enumerate((self.x, self.xb, self.xf, self.xo)):
            swaps[i].wait_send()
            ref = self.out.at[x, 1 - self.core]
            if i in (1, 2):
                ref = self.out.at[self.xf if i == 1 else self.xb, 1 - self.core]
            self.copy(ref, ref, self.psend.at[i], self.precv.at[i], to).wait_recv()


def gather_sems(zs):
    return [
        pltpu.SemaphoreType.DMA((2, zs // 2)),
        pltpu.SemaphoreType.DMA((2, zs // 2)),
        pltpu.SemaphoreType.DMA,
        pltpu.SemaphoreType.DMA((zs,)),
        pltpu.SemaphoreType.DMA((4,)),
        pltpu.SemaphoreType.DMA((4,)),
        pltpu.SemaphoreType.DMA((4,)),
        pltpu.SemaphoreType.DMA,
    ]


def greet(partners):
    barrier = pltpu.get_barrier_semaphore()
    for to in partners:
        pl.semaphore_signal(barrier, inc=1, device_id=to, device_id_type=MESH)
    pl.semaphore_wait(barrier, len(partners))


def gather_kernel(zs, own_ref, out_ref, *sems):
    moves = Gather(zs, own_ref, out_ref, sems[:-1])
    greet(moves.partners())
    moves.run(sems[-1])


def halves(first, second):
    pair = jnp.stack([first, second])
    pad = jnp.pad(pair, ((0, 0), (0, 2 * HALF - first.shape[0]), (0, 0)))
    return pad.reshape(2, 2, HALF, first.shape[1])


def whole_pair(out, rows):
    _, _, zs, _, width = out.shape
    parts = out.reshape(2, 2, 2, zs, HALF, width)
    parts = jnp.transpose(parts, (1, 3, 0, 2, 4, 5)).reshape(2, zs * 2, 2 * HALF, width)
    return [parts[i, :, :rows].reshape(-1, width) for i in range(2)]


def gather_pair(first, second, collective_id):
    rows, width = first.shape
    zs = lax.axis_size("dp") // 2
    out = pl.pallas_call(
        functools.partial(gather_kernel, zs),
        out_shape=jax.ShapeDtypeStruct((4, 2, zs, HALF, width), first.dtype),
        in_specs=[pl.BlockSpec(memory_space=pltpu.VMEM)],
        out_specs=pl.BlockSpec(memory_space=pltpu.VMEM),
        scratch_shapes=gather_sems(zs),
        compiler_params=pltpu.CompilerParams(collective_id=collective_id, has_side_effects=True),
        name=f"gather_pair_{collective_id}",
    )(halves(first, second))
    return whole_pair(out, rows)


def place_rows(received, meta, span_count):
    targets = jnp.arange(span_count, dtype=jnp.int32)[:, None]
    picker = meta[:, 0][None, :] == targets
    placed = jnp.einsum(
        "jb,btc->jtc", picker.astype(jnp.bfloat16), received, preferred_element_type=jnp.float32
    ).astype(jnp.bfloat16)
    live_counts = jnp.sum(jnp.where(picker, meta[:, 1][None, :], 0), axis=1).astype(jnp.int32)
    return (placed, live_counts)


def route_table(dest_grp, dest_slot, valid, extra, group_count, capacity):
    entries = dest_grp.shape[0]
    order = jnp.arange(entries, dtype=jnp.int32)
    earlier = (
        valid[None, :]
        & (dest_grp[None, :] == dest_grp[:, None])
        & (order[None, :] < order[:, None])
    )
    rank = jnp.sum(earlier.astype(jnp.int32), axis=1)
    bucket = jnp.where(valid, dest_grp * capacity + rank, -1)
    picker = bucket[None, :] == jnp.arange(group_count * capacity, dtype=jnp.int32)[:, None]
    slot_sent = jnp.sum(jnp.where(picker, dest_slot[None, :] + 1, 0), axis=1) - 1
    extra_sent = jnp.sum(jnp.where(picker, extra[None, :], 0), axis=1)
    meta = jnp.stack([slot_sent, extra_sent], axis=1)
    return (picker, meta)


def bucket_rows(rows, owner, extra, group_count, dp_count):
    span_count = owner.shape[0]
    dest_grp = owner // span_count // dp_count
    dest_slot = owner % span_count
    valid = jnp.ones((span_count,), dtype=bool)
    picker, meta = route_table(dest_grp, dest_slot, valid, extra, group_count, span_count // 2)
    packed = jnp.einsum(
        "bj,jtc->btc", picker.astype(jnp.bfloat16), rows, preferred_element_type=jnp.float32
    ).astype(jnp.bfloat16)
    return (packed, meta)


def attend_local(query_blocks, keys, values, live_counts):
    key_len = keys.shape[1]
    scores = jnp.einsum(
        "cqhd,ckhd->chqk", query_blocks, keys, preferred_element_type=jnp.float32
    ) * HEAD ** (-0.5)
    position = jnp.arange(key_len, dtype=jnp.int32) // NLEN
    live = (position[None, :] < live_counts[:, None])[:, None, None, :]
    masked = jnp.where(live, scores, -1e30)
    top = jnp.maximum(jnp.max(masked, axis=-1), 0.0)
    probs = jnp.where(live, jnp.exp(masked - top[..., None]), 0.0)
    denom = jnp.sum(probs, axis=-1) + jnp.exp(-top)
    weights = probs.astype(jnp.bfloat16)
    mixed = jnp.einsum("chqk,ckhd->cqhd", weights, values, preferred_element_type=jnp.float32)
    mixed = mixed / jnp.transpose(denom, (0, 2, 1))[..., None]
    span_count, span_len = (mixed.shape[0], mixed.shape[1])
    return mixed.astype(jnp.bfloat16).reshape(span_count, span_len, -1)


def on_device(neighbours, counts, owner, norm_gain, w_in, w_out, w_key, w_value, queries):
    span_count, key_len, enc_width = neighbours.shape
    group_count = lax.axis_size("grp")
    dp_count = lax.axis_size("dp")
    local_width = queries.shape[1]
    query_rows = queries.reshape(span_count, -1, local_width)
    flat = neighbours.astype(jnp.float32).reshape(-1, enc_width)
    meansq = jnp.mean(flat * flat, axis=-1, keepdims=True)
    normed = (flat * lax.rsqrt(meansq + 1e-06) * norm_gain).astype(jnp.bfloat16)
    full_in, full_out = gather_pair(w_in, w_out.T, 0)
    pre = jnp.dot(normed, full_in, preferred_element_type=jnp.float32)
    hidden = jax.nn.gelu(pre, approximate=False).astype(jnp.bfloat16)
    partial_out = jnp.dot(
        hidden, full_out.T, preferred_element_type=jnp.float32
    )
    total = lax.psum(partial_out, "mp")
    states = (flat + total).astype(jnp.bfloat16).reshape(span_count, key_len, enc_width)
    packed, meta = bucket_rows(states, owner, counts, group_count, dp_count)
    received, received_meta = (
        lax.all_to_all(packed, "grp", split_axis=0, concat_axis=0, tiled=True),
        lax.all_to_all(meta, "grp", split_axis=0, concat_axis=0, tiled=True),
    )
    served, live_counts = place_rows(received, received_meta, span_count)
    served_flat = served.reshape(-1, enc_width)
    full_key, full_value = gather_pair(w_key, w_value, 1)
    key_total = jnp.dot(served_flat, full_key, preferred_element_type=jnp.float32)
    value_total = jnp.dot(served_flat, full_value, preferred_element_type=jnp.float32)
    heads = w_key.shape[1] // HEAD
    keys = key_total.astype(jnp.bfloat16).reshape(span_count, key_len, heads, HEAD)
    values = value_total.astype(jnp.bfloat16).reshape(span_count, key_len, heads, HEAD)
    query_blocks = query_rows.reshape(span_count, -1, heads, HEAD)
    mixed = attend_local(query_blocks, keys, values, live_counts)
    return mixed.reshape(queries.shape[0], queries.shape[1])


def solution(mesh):
    placed = (
        P(("grp", "dp"), None, None),
        P(("grp", "dp")),
        P(("grp", "dp")),
        P(),
        P("dp", "mp"),
        P("mp", "dp"),
        P("dp", "mp"),
        P("dp", "mp"),
        P(("grp", "dp"), "mp"),
    )
    return jax.shard_map(
        on_device, mesh=mesh, in_specs=placed, out_specs=P(("grp", "dp"), "mp"), check_vma=False
    )
```

```python
import functools

import jax
import jax.numpy as jnp
from jax import lax
from jax.experimental import pallas as pl
from jax.experimental.pallas import tpu as pltpu
from jax.sharding import PartitionSpec as P

HEAD = 128
NLEN = 128
MESH = pl.DeviceIdType.MESH
HALF = 16


def ring_place():
    g, d, m = (lax.axis_index(name) for name in ("grp", "dp", "mp"))
    core, x, z = g % 2, (d % 2) * 2 + g // 2, d // 2
    return core, x, z, m


def chip_core(x, core, z, m):
    return ((x % 2) * 2 + core, z * 2 + x // 2, m)


class Gather:
    def __init__(self, zs, own_ref, out_ref, sems):
        self.zs, self.out = zs, out_ref
        (self.zsend, self.zrecv, self.fsend, self.frecv, self.one, self.psend, self.precv) = sems
        self.core, self.x, self.z, self.m = ring_place()
        turn = 1 - 2 * self.core
        self.xf, self.xb = (self.x + 4 + turn) % 4, (self.x + 4 - turn) % 4
        self.xo = (self.x + 2) % 4
        self.own = own_ref.at[self.x % 2, self.core]

    def partners(self):
        z, zs = self.z, self.zs
        return [
            chip_core(self.x, self.core, (z + 1) % zs, self.m),
            chip_core(self.x, self.core, (z + zs - 1) % zs, self.m),
            chip_core(self.xf, self.core, z, self.m),
            chip_core(self.xb, self.core, z, self.m),
            chip_core(self.x, 1 - self.core, z, self.m),
        ]

    def copy(self, src, dst, send, recv, to):
        return pltpu.make_async_remote_copy(
            src_ref=src, dst_ref=dst, send_sem=send, recv_sem=recv, device_id=to, device_id_type=MESH
        )

    def slot(self, x, z):
        return self.out.at[x, self.core, z]

    def piece(self, x):
        return self.out.at[x, self.core]

    def ring(self, plus, s):
        zs = self.zs
        at = (self.z + zs - s) % zs if plus else (self.z + s) % zs
        to = self.partners()[0 if plus else 1]
        src = self.own if s == 0 else self.slot(self.x, at)
        row = 0 if plus else 1
        return self.copy(src, self.slot(self.x, at), self.zsend.at[row, s], self.zrecv.at[row, s], to)

    def arrived(self, plus, s):
        zs = self.zs
        at = (self.z + zs - s) % zs if plus else (self.z + s) % zs
        row = 0 if plus else 1
        ref = self.slot(self.x, at)
        self.copy(ref, ref, self.zsend.at[row, s - 1], self.zrecv.at[row, s - 1], self.partners()[0]).wait_recv()

    def across(self, at, j, own):
        src = self.own if own else self.slot(self.x, at)
        dst = self.slot(self.x, at)
        to = self.partners()
        self.copy(src, dst, self.fsend, self.frecv.at[j], to[2]).start()
        self.copy(src, dst, self.one.at[0], self.one.at[1], to[3]).start()

    def relay(self, at, j):
        ref = self.slot(self.xb, at)
        self.copy(ref, ref, self.fsend, self.frecv.at[j], self.partners()[2]).wait_recv()
        self.copy(ref, ref, self.one.at[2], self.one.at[3], self.partners()[2]).start()

    def fresh(self, s):
        zs = self.zs
        if s == 0:
            return [(self.z, 0)]
        found = [((self.z + zs - s) % zs, 2 * s - 1)]
        if s <= (zs - 1) // 2:
            found.append(((self.z + s) % zs, 2 * s))
        return found

    def run(self, local):
        last, back = self.zs // 2, (self.zs - 1) // 2
        keep = pltpu.make_async_copy(self.own, self.slot(self.x, self.z), local)
        keep.start()
        for s in range(last + 1):
            if s > 0:
                self.arrived(True, s)
            if s < last:
                self.ring(True, s).start()
            if 0 < s <= back:
                self.arrived(False, s)
            if s < back:
                self.ring(False, s).start()
            for at, j in self.fresh(s):
                self.across(at, j, s == 0)
            if s > 0:
                for at, j in self.fresh(s - 1):
                    self.relay(at, j)
        keep.wait()
        to = self.partners()[4]
        swaps = []

        def swap(x):
            ref = self.piece(x)
            i = len(swaps)
            swaps.append(self.copy(ref, ref, self.psend.at[i], self.precv.at[i], to))
            swaps[-1].start()

        swap(self.x)
        for at, j in self.fresh(last):
            self.relay(at, j)
        swap(self.xb)
        whole = self.piece(self.xf)
        self.copy(whole, whole, self.one.at[0], self.one.at[1], to).wait_recv()
        swap(self.xf)
        whole = self.piece(self.xo)
        self.copy(whole, whole, self.one.at[2], self.one.at[3], to).wait_recv()
        swap(self.xo)
        for s in range(last):
            self.ring(True, s).wait_send()
            if s < back:
                self.ring(False, s).wait_send()
        whole = self.piece(self.x)
        for sem in (self.fsend, self.one.at[0], self.one.at[2]):
            self.copy(whole, whole, sem, self.one.at[1], to).wait_send()
        for i, x in enumerate((self.x, self.xb, self.xf, self.xo)):
            swaps[i].wait_send()
            ref = self.out.at[x, 1 - self.core]
            if i in (1, 2):
                ref = self.out.at[self.xf if i == 1 else self.xb, 1 - self.core]
            self.copy(ref, ref, self.psend.at[i], self.precv.at[i], to).wait_recv()


def gather_sems(zs):
    return [
        pltpu.SemaphoreType.DMA((2, zs // 2)),
        pltpu.SemaphoreType.DMA((2, zs // 2)),
        pltpu.SemaphoreType.DMA,
        pltpu.SemaphoreType.DMA((zs,)),
        pltpu.SemaphoreType.DMA((4,)),
        pltpu.SemaphoreType.DMA((4,)),
        pltpu.SemaphoreType.DMA((4,)),
        pltpu.SemaphoreType.DMA,
    ]


def greet(partners):
    barrier = pltpu.get_barrier_semaphore()
    for to in partners:
        pl.semaphore_signal(barrier, inc=1, device_id=to, device_id_type=MESH)
    pl.semaphore_wait(barrier, len(partners))


def beside(x):
    return x + 1 - 2 * (x % 2)


def gather_kernel(zs, own_ref, note_ref, out_ref, notes_ref, *sems):
    moves = Gather(zs, own_ref, out_ref, sems[:-4])
    core, x, z, m = ring_place()
    near = [
        chip_core(x, 1 - core, z, m),
        chip_core(beside(x), core, z, m),
        chip_core(beside(x), 1 - core, z, m),
    ]
    nsend, nrecv, nlocal = sems[-4:-1]
    g = lax.axis_index("grp")
    greet(moves.partners() + near[2:])
    keep = pltpu.make_async_copy(note_ref, notes_ref.at[g], nlocal)
    keep.start()
    told = []
    for i, to in enumerate(near):
        told.append(moves.copy(note_ref, notes_ref.at[g], nsend.at[i], nrecv.at[i], to))
        told[-1].start()
    moves.run(sems[-1])
    keep.wait()
    for i, copy in enumerate(told):
        copy.wait_send()
        from_core = core if i == 1 else 1 - core
        from_low = x % 2 if i == 0 else 1 - x % 2
        ref = notes_ref.at[from_low * 2 + from_core]
        moves.copy(ref, ref, nsend.at[i], nrecv.at[i], near[i]).wait_recv()


class Ring(Gather):
    def slot(self, x, z):
        return self.out.at[z]

    def run(self, local, between):
        last, back = self.zs // 2, (self.zs - 1) // 2
        keep = pltpu.make_async_copy(self.own, self.slot(self.x, self.z), local)
        keep.start()
        for s in range(last + 1):
            if s > 0:
                self.arrived(True, s)
            if s < last:
                self.ring(True, s).start()
            if 0 < s <= back:
                self.arrived(False, s)
            if s < back:
                self.ring(False, s).start()
            if s == last // 2:
                between()
        keep.wait()
        for s in range(last):
            self.ring(True, s).wait_send()
            if s < back:
                self.ring(False, s).wait_send()


def sums_kernel(zs, own_ref, part_ref, out_ref, got_ref, relay, ysend, yrecv, zsend, zrecv, local):
    moves = Ring(zs, own_ref, out_ref, (zsend, zrecv) + (None,) * 5)
    core, x, z, m = ring_place()
    up, down, far = (m + 1) % 4, (m + 3) % 4, (m + 2) % 4
    to_up, to_down = chip_core(x, core, z, up), chip_core(x, core, z, down)
    greet(moves.partners()[:2] + [to_up, to_down])

    def make(i, src, dst, to):
        return moves.copy(src, dst, ysend.at[i], yrecv.at[i], to)

    low, high = pl.ds(0, 2), pl.ds(2, 2)
    copies = [
        make(0, part_ref.at[low, far], relay.at[0], to_up),
        make(1, part_ref.at[high, far], relay.at[1], to_down),
        make(2, part_ref.at[:, up], got_ref.at[0], to_up),
        make(3, part_ref.at[:, down], got_ref.at[1], to_down),
        make(4, relay.at[0], got_ref.at[2, low], to_up),
        make(5, relay.at[1], got_ref.at[2, high], to_down),
    ]
    for copy in copies[:4]:
        copy.start()

    def pass_on():
        for i in range(2):
            copies[i].wait_recv()
            copies[4 + i].start()

    moves.run(local, pass_on)
    for i, copy in enumerate(copies):
        copy.wait_send()
        if i >= 2:
            copy.wait_recv()


def route_kernel(zs, owner_ref, states_ref, piece_ref, full_ref, out_ref, send, cand, rsend, rrecv, ysend, yrecv, xsend, xrecv, psend, precv, local):
    core, x, z, m = ring_place()
    g, d = lax.axis_index("grp"), lax.axis_index("dp")
    turn = 1 - 2 * core
    xf, xb, xo = (x + 4 + turn) % 4, (x + 4 - turn) % 4, (x + 2) % 4
    up, down, far = (m + 1) % 4, (m + 3) % 4, (m + 2) % 4
    to_up, to_down = chip_core(x, core, z, up), chip_core(x, core, z, down)
    to_f, to_b = chip_core(xf, core, z, m), chip_core(xb, core, z, m)
    to_core, to_side = chip_core(x, 1 - core, z, m), chip_core(beside(x), core, z, m)
    spans, block = 4, 4 * lax.axis_size("dp")

    def copy(src, dst, sends, recvs, i, to):
        return pltpu.make_async_remote_copy(
            src_ref=src, dst_ref=dst, send_sem=sends.at[i], recv_sem=recvs.at[i], device_id=to, device_id_type=MESH
        )

    picks = [jnp.int32(0)] * 2
    finds = [jnp.int32(0)] * spans
    for source in range(4):
        low_gap = jnp.where(g // 2 == source // 2, 0, 2)
        apart = low_gap + jnp.where(core == source % 2, 0, 1)
        rank = jnp.int32(0)
        for i in range(spans):
            target = owner_ref[source * spans + i]
            leaves = (target < source * block) | (target >= (source + 1) * block)
            for r in range(2):
                picks[r] = jnp.where(leaves & (rank == r) & (apart == 0), i, picks[r])
            spot = jnp.where(apart == 0, i, 4 + 2 * (apart - 1) + jnp.minimum(rank, 1))
            for j in range(spans):
                mine = target == (g * lax.axis_size("dp") + d) * spans + j
                finds[j] = jnp.where(mine, spot, finds[j])
            rank = rank + jnp.where(leaves, 1, 0)

    for r in range(2):
        send[r] = states_ref[picks[r]]
    greet([to_f, to_b, to_core, to_up, to_down])
    first = [
        copy(send, cand.at[pl.ds(4, 2)], rsend, rrecv, 0, to_core),
        copy(send, cand.at[pl.ds(6, 2)], rsend, rrecv, 1, to_side),
        copy(cand.at[pl.ds(6, 2)], cand.at[pl.ds(8, 2)], rsend, rrecv, 2, to_core),
    ]
    first[1].start()
    first[0].start()
    held = pltpu.make_async_copy(states_ref, cand.at[pl.ds(0, 4)], local.at[0])
    held.start()
    keep = pltpu.make_async_copy(piece_ref, out_ref.at[x, core], local.at[1])
    keep.start()
    here = out_ref.at[x, core]
    back, front, over = out_ref.at[xb, core], out_ref.at[xf, core], out_ref.at[xo, core]
    to_front = copy(piece_ref, here, xsend, xrecv, 0, to_f)
    to_back = copy(piece_ref, here, xsend, xrecv, 1, to_b)
    onward = copy(back, back, xsend, xrecv, 2, to_f)
    to_front.start()
    to_back.start()
    first[1].wait_recv()
    first[2].start()
    first[0].wait_recv()
    held.wait()
    first[2].wait_recv()
    for j in range(spans):
        full_ref[j, m] = cand[finds[j]]

    low, high = pl.ds(0, 2), pl.ds(2, 2)

    def share(i, rows, of, to):
        ref = full_ref.at[rows, of]
        return copy(ref, ref, ysend, yrecv, i, to)

    shares = [
        share(0, low, m, to_up),
        share(1, high, m, to_down),
        share(2, high, m, to_up),
        share(3, low, m, to_down),
        share(4, low, down, to_up),
        share(5, high, up, to_down),
    ]
    arrivals = [
        share(0, low, down, to_up),
        share(1, high, up, to_down),
        share(2, high, down, to_up),
        share(3, low, up, to_down),
        share(4, low, far, to_up),
        share(5, high, far, to_down),
    ]
    for one in shares[:4]:
        one.start()
    for i in range(2):
        arrivals[i].wait_recv()
        shares[4 + i].start()

    keep.wait()
    swaps = [copy(ref, ref, psend, precv, i, to_core) for i, ref in enumerate((here, back, front, over))]
    swaps[0].start()
    copy(back, back, xsend, xrecv, 0, to_f).wait_recv()
    onward.start()
    swaps[1].start()
    copy(front, front, xsend, xrecv, 1, to_b).wait_recv()
    swaps[2].start()
    copy(over, over, xsend, xrecv, 2, to_f).wait_recv()
    swaps[3].start()
    for one in arrivals[2:]:
        one.wait_recv()
    for one in shares + first + [to_front, to_back, onward] + swaps:
        one.wait_send()
    for i, at in enumerate((x, xf, xb, xo)):
        ref = out_ref.at[at, 1 - core]
        copy(ref, ref, psend, precv, i, to_core).wait_recv()


def halves(first, second):
    pair = jnp.stack([first, second])
    pad = jnp.pad(pair, ((0, 0), (0, 2 * HALF - first.shape[0]), (0, 0)))
    return pad.reshape(2, 2, HALF, first.shape[1])


def whole_pair(out, rows):
    _, _, zs, _, width = out.shape
    parts = out.reshape(2, 2, 2, zs, HALF, width)
    parts = jnp.transpose(parts, (1, 3, 0, 2, 4, 5)).reshape(2, zs * 2, 2 * HALF, width)
    return [parts[i, :, :rows].reshape(-1, width) for i in range(2)]


def call(body, ins, outs, scratch, collective_id, name):
    return pl.pallas_call(
        body,
        out_shape=outs,
        in_specs=[pl.BlockSpec(memory_space=space) for space in ins],
        out_specs=[pl.BlockSpec(memory_space=pltpu.VMEM)] * len(outs),
        scratch_shapes=scratch,
        compiler_params=pltpu.CompilerParams(collective_id=collective_id, has_side_effects=True),
        name=name,
    )


def dma(*shape):
    return pltpu.SemaphoreType.DMA(shape)


def gather_first(first, second, note):
    rows, width = first.shape
    zs = lax.axis_size("dp") // 2
    outs = [
        jax.ShapeDtypeStruct((4, 2, zs, HALF, width), first.dtype),
        jax.ShapeDtypeStruct((4,) + note.shape, note.dtype),
    ]
    sems = gather_sems(zs)
    sems[-1:] = [dma(3), dma(3), pltpu.SemaphoreType.DMA, pltpu.SemaphoreType.DMA]
    body = functools.partial(gather_kernel, zs)
    out, notes = call(body, [pltpu.VMEM] * 2, outs, sems, 0, "gather_first")(halves(first, second), note)
    return whole_pair(out, rows), notes


def sum_over_units(parts, key_value):
    zs = lax.axis_size("dp") // 2
    spans, _, rows, width = parts.shape
    outs = [
        jax.ShapeDtypeStruct((zs,) + key_value.shape[2:], key_value.dtype),
        jax.ShapeDtypeStruct((3, spans, rows, width), parts.dtype),
    ]
    scratch = [pltpu.VMEM((2, 2, rows, width), parts.dtype), dma(6), dma(6)]
    scratch += [dma(2, zs // 2), dma(2, zs // 2), pltpu.SemaphoreType.DMA]
    body = functools.partial(sums_kernel, zs)
    return call(body, [pltpu.VMEM] * 2, outs, scratch, 1, "sum_over_units")(key_value, parts)


def route_states(owners, states, piece):
    zs = piece.shape[0]
    spans, rows, width = states.shape
    outs = [
        jax.ShapeDtypeStruct((spans, 4, rows, width), states.dtype),
        jax.ShapeDtypeStruct((4, 2) + piece.shape, piece.dtype),
    ]
    scratch = [pltpu.VMEM((2, rows, width), states.dtype), pltpu.VMEM((10, rows, width), states.dtype)]
    scratch += [dma(3), dma(3), dma(6), dma(6), dma(3), dma(3), dma(4), dma(4), dma(2)]
    body = functools.partial(route_kernel, zs)
    ins = [pltpu.SMEM, pltpu.VMEM, pltpu.VMEM]
    return call(body, ins, outs, scratch, 2, "route_states")(owners, states, piece)


def attend_local(query_blocks, keys, values, live_counts):
    key_len = keys.shape[1]
    scores = jnp.einsum(
        "cqhd,ckhd->chqk", query_blocks, keys, preferred_element_type=jnp.float32
    ) * HEAD ** (-0.5)
    position = jnp.arange(key_len, dtype=jnp.int32) // NLEN
    live = (position[None, :] < live_counts[:, None])[:, None, None, :]
    masked = jnp.where(live, scores, -1e30)
    top = jnp.maximum(jnp.max(masked, axis=-1), 0.0)
    probs = jnp.where(live, jnp.exp(masked - top[..., None]), 0.0)
    denom = jnp.sum(probs, axis=-1) + jnp.exp(-top)
    weights = probs.astype(jnp.bfloat16)
    mixed = jnp.einsum("chqk,ckhd->cqhd", weights, values, preferred_element_type=jnp.float32)
    mixed = mixed / jnp.transpose(denom, (0, 2, 1))[..., None]
    span_count, span_len = (mixed.shape[0], mixed.shape[1])
    return mixed.astype(jnp.bfloat16).reshape(span_count, span_len, -1)


def on_device(neighbours, counts, owner, norm_gain, w_in, w_out, w_key, w_value, queries):
    span_count, key_len, enc_width = neighbours.shape
    dp_count, m = lax.axis_size("dp"), lax.axis_index("mp")
    local_width = queries.shape[1]
    query_rows = queries.reshape(span_count, -1, local_width)
    note = jnp.pad(jnp.stack([owner, counts]), ((0, 6), (0, 128 - span_count)))
    (full_in, full_out), notes = gather_first(w_in, w_out.T, note)
    flat = neighbours.astype(jnp.float32).reshape(-1, enc_width)
    meansq = jnp.mean(flat * flat, axis=-1, keepdims=True)
    normed = (flat * lax.rsqrt(meansq + 1e-06) * norm_gain).astype(jnp.bfloat16)
    pre = jnp.dot(normed, full_in, preferred_element_type=jnp.float32)
    hidden = jax.nn.gelu(pre, approximate=False).astype(jnp.bfloat16)
    partial_out = jnp.dot(hidden, full_out.T, preferred_element_type=jnp.float32)
    parts = partial_out.astype(jnp.bfloat16).reshape(span_count, 4, key_len // 4, enc_width)
    piece, got = sum_over_units(parts, halves(w_key, w_value))
    own = lax.dynamic_index_in_dim(parts, m, 1, keepdims=False).astype(jnp.float32)
    rows = neighbours.reshape(parts.shape)
    rows = lax.dynamic_index_in_dim(rows, m, 1, keepdims=False).astype(jnp.float32)
    got = got.astype(jnp.float32)
    states = (rows + (own + got[0] + got[1] + got[2])).astype(jnp.bfloat16)
    owners = notes[:, 0, :span_count].reshape(-1)
    senders = notes[:, 1, :span_count].reshape(-1)
    served, pair = route_states(owners, states, piece)
    full_key, full_value = whole_pair(pair, w_key.shape[0])
    first_block = (lax.axis_index("grp") * dp_count + lax.axis_index("dp")) * span_count
    slots = first_block + jnp.arange(span_count, dtype=jnp.int32)
    live_counts = jnp.sum(jnp.where(owners[None] == slots[:, None], senders[None], 0), axis=1)
    served_flat = served.reshape(-1, enc_width)
    key_total = jnp.dot(served_flat, full_key, preferred_element_type=jnp.float32)
    value_total = jnp.dot(served_flat, full_value, preferred_element_type=jnp.float32)
    heads = w_key.shape[1] // HEAD
    keys = key_total.astype(jnp.bfloat16).reshape(span_count, key_len, heads, HEAD)
    values = value_total.astype(jnp.bfloat16).reshape(span_count, key_len, heads, HEAD)
    query_blocks = query_rows.reshape(span_count, -1, heads, HEAD)
    mixed = attend_local(query_blocks, keys, values, live_counts)
    return mixed.reshape(queries.shape[0], queries.shape[1])


def solution(mesh):
    placed = (
        P(("grp", "dp"), None, None),
        P(("grp", "dp")),
        P(("grp", "dp")),
        P(),
        P("dp", "mp"),
        P("mp", "dp"),
        P("dp", "mp"),
        P("dp", "mp"),
        P(("grp", "dp"), "mp"),
    )
    return jax.shard_map(
        on_device, mesh=mesh, in_specs=placed, out_specs=P(("grp", "dp"), "mp"), check_vma=False
    )
```

```python
import functools

import jax
import jax.numpy as jnp
from jax import lax
from jax.experimental import pallas as pl
from jax.experimental.pallas import tpu as pltpu
from jax.sharding import PartitionSpec as P

HEAD = 128
NLEN = 128
MESH = pl.DeviceIdType.MESH
HALF = 16


def ring_place():
    g, d, m = (lax.axis_index(name) for name in ("grp", "dp", "mp"))
    core, x, z = g % 2, (d % 2) * 2 + g // 2, d // 2
    return core, x, z, m


def chip_core(x, core, z, m):
    return ((x % 2) * 2 + core, z * 2 + x // 2, m)


class Gather:
    def __init__(self, zs, own_ref, out_ref, sems):
        self.zs, self.out = zs, out_ref
        (self.zsend, self.zrecv, self.fsend, self.frecv, self.one, self.psend, self.precv) = sems
        self.core, self.x, self.z, self.m = ring_place()
        turn = 1 - 2 * self.core
        self.xf, self.xb = (self.x + 4 + turn) % 4, (self.x + 4 - turn) % 4
        self.xo = (self.x + 2) % 4
        self.own = own_ref.at[self.x % 2, self.core]

    def partners(self):
        z, zs = self.z, self.zs
        return [
            chip_core(self.x, self.core, (z + 1) % zs, self.m),
            chip_core(self.x, self.core, (z + zs - 1) % zs, self.m),
            chip_core(self.xf, self.core, z, self.m),
            chip_core(self.xb, self.core, z, self.m),
            chip_core(self.x, 1 - self.core, z, self.m),
        ]

    def copy(self, src, dst, send, recv, to):
        return pltpu.make_async_remote_copy(
            src_ref=src, dst_ref=dst, send_sem=send, recv_sem=recv, device_id=to, device_id_type=MESH
        )

    def slot(self, x, z):
        return self.out.at[x, self.core, z]

    def piece(self, x):
        return self.out.at[x, self.core]

    def ring(self, plus, s):
        zs = self.zs
        at = (self.z + zs - s) % zs if plus else (self.z + s) % zs
        to = self.partners()[0 if plus else 1]
        src = self.own if s == 0 else self.slot(self.x, at)
        row = 0 if plus else 1
        return self.copy(src, self.slot(self.x, at), self.zsend.at[row, s], self.zrecv.at[row, s], to)

    def arrived(self, plus, s):
        zs = self.zs
        at = (self.z + zs - s) % zs if plus else (self.z + s) % zs
        row = 0 if plus else 1
        ref = self.slot(self.x, at)
        self.copy(ref, ref, self.zsend.at[row, s - 1], self.zrecv.at[row, s - 1], self.partners()[0]).wait_recv()

    def across(self, at, j, own):
        src = self.own if own else self.slot(self.x, at)
        dst = self.slot(self.x, at)
        to = self.partners()
        self.copy(src, dst, self.fsend, self.frecv.at[j], to[2]).start()
        self.copy(src, dst, self.one.at[0], self.one.at[1], to[3]).start()

    def relay(self, at, j):
        ref = self.slot(self.xb, at)
        self.copy(ref, ref, self.fsend, self.frecv.at[j], self.partners()[2]).wait_recv()
        self.copy(ref, ref, self.one.at[2], self.one.at[3], self.partners()[2]).start()

    def fresh(self, s):
        zs = self.zs
        if s == 0:
            return [(self.z, 0)]
        found = [((self.z + zs - s) % zs, 2 * s - 1)]
        if s <= (zs - 1) // 2:
            found.append(((self.z + s) % zs, 2 * s))
        return found

    def run(self, local, also):
        last, back = self.zs // 2, (self.zs - 1) // 2
        keep = pltpu.make_async_copy(self.own, self.slot(self.x, self.z), local)
        keep.start()
        for s in range(last + 1):
            if s > 0:
                self.arrived(True, s)
            if s < last:
                self.ring(True, s).start()
            if 0 < s <= back:
                self.arrived(False, s)
            if s < back:
                self.ring(False, s).start()
            also.step(s)
            for at, j in self.fresh(s):
                self.across(at, j, s == 0)
            if s > 0:
                for at, j in self.fresh(s - 1):
                    self.relay(at, j)
        keep.wait()
        to = self.partners()[4]
        swaps = []

        def swap(x):
            ref = self.piece(x)
            i = len(swaps)
            swaps.append(self.copy(ref, ref, self.psend.at[i], self.precv.at[i], to))
            swaps[-1].start()

        swap(self.x)
        for at, j in self.fresh(last):
            self.relay(at, j)
        swap(self.xb)
        whole = self.piece(self.xf)
        self.copy(whole, whole, self.one.at[0], self.one.at[1], to).wait_recv()
        swap(self.xf)
        whole = self.piece(self.xo)
        self.copy(whole, whole, self.one.at[2], self.one.at[3], to).wait_recv()
        swap(self.xo)
        for s in range(last):
            self.ring(True, s).wait_send()
            if s < back:
                self.ring(False, s).wait_send()
        whole = self.piece(self.x)
        for sem in (self.fsend, self.one.at[0], self.one.at[2]):
            self.copy(whole, whole, sem, self.one.at[1], to).wait_send()
        for i, x in enumerate((self.x, self.xb, self.xf, self.xo)):
            swaps[i].wait_send()
            ref = self.out.at[x, 1 - self.core]
            if i in (1, 2):
                ref = self.out.at[self.xf if i == 1 else self.xb, 1 - self.core]
            self.copy(ref, ref, self.psend.at[i], self.precv.at[i], to).wait_recv()


def gather_sems(zs):
    return [
        pltpu.SemaphoreType.DMA((2, zs // 2)),
        pltpu.SemaphoreType.DMA((2, zs // 2)),
        pltpu.SemaphoreType.DMA,
        pltpu.SemaphoreType.DMA((zs,)),
        pltpu.SemaphoreType.DMA((4,)),
        pltpu.SemaphoreType.DMA((4,)),
        pltpu.SemaphoreType.DMA((4,)),
        pltpu.SemaphoreType.DMA,
    ]


def greet(partners):
    barrier = pltpu.get_barrier_semaphore()
    for to in partners:
        pl.semaphore_signal(barrier, inc=1, device_id=to, device_id_type=MESH)
    pl.semaphore_wait(barrier, len(partners))


def beside(x):
    return x + 1 - 2 * (x % 2)


class Ring(Gather):
    def __init__(self, zs, own_ref, out_ref, sems, local):
        super().__init__(zs, own_ref, out_ref, sems + (None,) * 5)
        self.local = local

    def slot(self, x, z):
        return self.out.at[z]

    def kept(self):
        return pltpu.make_async_copy(self.own, self.slot(self.x, self.z), self.local)

    def step(self, s):
        last, back = self.zs // 2, (self.zs - 1) // 2
        if s > 0:
            self.arrived(True, s)
        if s < last:
            self.ring(True, s).start()
        if 0 < s <= back:
            self.arrived(False, s)
        if s < back:
            self.ring(False, s).start()

    def finish(self):
        self.kept().wait()
        for s in range(self.zs // 2):
            self.ring(True, s).wait_send()
            if s < (self.zs - 1) // 2:
                self.ring(False, s).wait_send()


def unpad(zs, held_ref, full_refs):
    rows = full_refs[0].shape[0] // (2 * zs)
    for a, full in enumerate(full_refs):
        for z in range(zs):
            for high in range(2):
                at = (2 * z + high) * rows
                full[at : at + HALF] = held_ref[high * 2 + a, 0, z]
                full[at + HALF : at + rows] = held_ref[high * 2 + a, 1, z, : rows - HALF]


def gather_kernel(zs, own_ref, later_ref, note_ref, in_ref, out_ref, piece_ref, notes_ref, held, *sems):
    moves = Gather(zs, own_ref, held, sems[:7])
    also = Ring(zs, later_ref, piece_ref, sems[8:10], sems[10])
    nsend, nrecv, nlocal = sems[11:]
    core, x, z, m = ring_place()
    near = [
        chip_core(x, 1 - core, z, m),
        chip_core(beside(x), core, z, m),
        chip_core(beside(x), 1 - core, z, m),
    ]
    g = lax.axis_index("grp")
    greet(moves.partners() + near[2:])
    keep = pltpu.make_async_copy(note_ref, notes_ref.at[g], nlocal)
    keep.start()
    also.kept().start()
    told = []
    for i, to in enumerate(near):
        told.append(moves.copy(note_ref, notes_ref.at[g], nsend.at[i], nrecv.at[i], to))
        told[-1].start()
    moves.run(sems[7], also)
    unpad(zs, held, (in_ref, out_ref))
    also.finish()
    keep.wait()
    for i, copy in enumerate(told):
        copy.wait_send()
        from_core = core if i == 1 else 1 - core
        from_low = x % 2 if i == 0 else 1 - x % 2
        ref = notes_ref.at[from_low * 2 + from_core]
        moves.copy(ref, ref, nsend.at[i], nrecv.at[i], near[i]).wait_recv()


def remote(src, dst, sends, recvs, i, to):
    return pltpu.make_async_remote_copy(
        src_ref=src, dst_ref=dst, send_sem=sends.at[i], recv_sem=recvs.at[i], device_id=to, device_id_type=MESH
    )


def sums_kernel(zs, piece_ref, part_ref, key_ref, value_ref, got_ref, held, relay, ysend, yrecv, xsend, xrecv, psend, precv, local):
    core, x, z, m = ring_place()
    turn = 1 - 2 * core
    xf, xb, xo = (x + 4 + turn) % 4, (x + 4 - turn) % 4, (x + 2) % 4
    up, down, far = (m + 1) % 4, (m + 3) % 4, (m + 2) % 4
    to_up, to_down = chip_core(x, core, z, up), chip_core(x, core, z, down)
    to_f, to_b = chip_core(xf, core, z, m), chip_core(xb, core, z, m)
    to_core = chip_core(x, 1 - core, z, m)
    greet([to_f, to_b, to_core, to_up, to_down])

    def make(i, src, dst, to):
        return remote(src, dst, ysend, yrecv, i, to)

    low, high = pl.ds(0, 2), pl.ds(2, 2)
    copies = [
        make(0, part_ref.at[low, far], relay.at[0], to_up),
        make(1, part_ref.at[high, far], relay.at[1], to_down),
        make(2, part_ref.at[:, up], got_ref.at[0], to_up),
        make(3, part_ref.at[:, down], got_ref.at[1], to_down),
        make(4, relay.at[0], got_ref.at[2, low], to_up),
        make(5, relay.at[1], got_ref.at[2, high], to_down),
    ]
    for copy in copies[:4]:
        copy.start()
    keep = pltpu.make_async_copy(piece_ref, held.at[x, core], local)
    keep.start()
    here = held.at[x, core]
    back, front, over = held.at[xb, core], held.at[xf, core], held.at[xo, core]
    to_front = remote(piece_ref, here, xsend, xrecv, 0, to_f)
    to_back = remote(piece_ref, here, xsend, xrecv, 1, to_b)
    onward = remote(back, back, xsend, xrecv, 2, to_f)
    to_front.start()
    to_back.start()
    swaps = [remote(ref, ref, psend, precv, i, to_core) for i, ref in enumerate((here, back, front, over))]
    keep.wait()
    swaps[0].start()
    for i in range(2):
        copies[i].wait_recv()
        copies[4 + i].start()
    remote(back, back, xsend, xrecv, 0, to_f).wait_recv()
    onward.start()
    swaps[1].start()
    remote(front, front, xsend, xrecv, 1, to_b).wait_recv()
    swaps[2].start()
    remote(over, over, xsend, xrecv, 2, to_f).wait_recv()
    swaps[3].start()
    for i, at in enumerate((x, xf, xb, xo)):
        ref = held.at[at, 1 - core]
        remote(ref, ref, psend, precv, i, to_core).wait_recv()
    unpad(zs, held, (key_ref, value_ref))
    for copy in copies[2:]:
        copy.wait_recv()
    for copy in copies + [to_front, to_back, onward] + swaps:
        copy.wait_send()


def route_kernel(owner_ref, count_ref, states_ref, key_ref, value_ref, query_ref, out_ref, send, cand, full_ref, keys, values, rsend, rrecv, ysend, yrecv, local):
    core, x, z, m = ring_place()
    g, d = lax.axis_index("grp"), lax.axis_index("dp")
    up, down, far = (m + 1) % 4, (m + 3) % 4, (m + 2) % 4
    to_up, to_down = chip_core(x, core, z, up), chip_core(x, core, z, down)
    to_core, to_side = chip_core(x, 1 - core, z, m), chip_core(beside(x), core, z, m)
    spans, block = 4, 4 * lax.axis_size("dp")

    picks = [jnp.int32(0)] * 2
    finds = [jnp.int32(0)] * spans
    lives = [jnp.int32(0)] * spans
    for source in range(4):
        low_gap = jnp.where(g // 2 == source // 2, 0, 2)
        apart = low_gap + jnp.where(core == source % 2, 0, 1)
        rank = jnp.int32(0)
        for i in range(spans):
            target = owner_ref[source * spans + i]
            leaves = (target < source * block) | (target >= (source + 1) * block)
            for r in range(2):
                picks[r] = jnp.where(leaves & (rank == r) & (apart == 0), i, picks[r])
            spot = jnp.where(apart == 0, i, 4 + 2 * (apart - 1) + jnp.minimum(rank, 1))
            for j in range(spans):
                mine = target == (g * lax.axis_size("dp") + d) * spans + j
                finds[j] = jnp.where(mine, spot, finds[j])
                lives[j] = jnp.where(mine, count_ref[source * spans + i], lives[j])
            rank = rank + jnp.where(leaves, 1, 0)

    for r in range(2):
        send[r] = states_ref[picks[r]]
    greet([to_core, to_side, to_up, to_down])
    first = [
        remote(send, cand.at[pl.ds(4, 2)], rsend, rrecv, 0, to_core),
        remote(send, cand.at[pl.ds(6, 2)], rsend, rrecv, 1, to_side),
        remote(cand.at[pl.ds(6, 2)], cand.at[pl.ds(8, 2)], rsend, rrecv, 2, to_core),
    ]
    first[1].start()
    first[0].start()
    held = pltpu.make_async_copy(states_ref, cand.at[pl.ds(0, 4)], local)
    held.start()
    first[1].wait_recv()
    first[2].start()
    first[0].wait_recv()
    held.wait()
    first[2].wait_recv()
    for j in range(spans):
        full_ref[j, m] = cand[finds[j]]

    low, high = pl.ds(0, 2), pl.ds(2, 2)

    def share(i, rows, of, to):
        ref = full_ref.at[rows, of]
        return remote(ref, ref, ysend, yrecv, i, to)

    shares = [
        share(0, low, m, to_up),
        share(1, high, m, to_down),
        share(2, high, m, to_up),
        share(3, low, m, to_down),
        share(4, low, down, to_up),
        share(5, high, up, to_down),
    ]
    arrivals = [
        share(0, low, down, to_up),
        share(1, high, up, to_down),
        share(2, high, down, to_up),
        share(3, low, up, to_down),
        share(4, low, far, to_up),
        share(5, high, far, to_down),
    ]
    for one in shares[:4]:
        one.start()
    project = functools.partial(project_rows, full_ref, ((key_ref, keys), (value_ref, values)))
    for i in range(2):
        arrivals[i].wait_recv()
        shares[4 + i].start()
    project(m)
    arrivals[2].wait_recv()
    project(down)
    arrivals[3].wait_recv()
    project(up)
    arrivals[4].wait_recv()
    arrivals[5].wait_recv()
    project(far)
    attend(query_ref, keys, values, lives, out_ref)
    for one in shares + first:
        one.wait_send()


def project_rows(full_ref, pairs, of):
    spans, _, rows, width = full_ref.shape
    block = full_ref[:, of].reshape(spans * rows, width)
    tile = min(256, pairs[0][0].shape[1])
    for weight, result in pairs:

        def column(t, carry, weight=weight, result=result):
            at = pl.ds(pl.multiple_of(t * tile, tile), tile)
            made = jnp.dot(block, weight[:, at], preferred_element_type=jnp.float32)
            result[:, of, :, at] = made.astype(result.dtype).reshape(spans, rows, tile)
            return carry

        lax.fori_loop(0, weight.shape[1] // tile, column, 0)


def attend(query_ref, keys, values, lives, out_ref):
    spans, quarters, rows, width = keys.shape
    length = quarters * rows
    lines = query_ref.shape[0] // spans
    position = lax.broadcasted_iota(jnp.int32, (lines, length), 1)

    def head(h, carry):
        at = pl.ds(pl.multiple_of(h * HEAD, HEAD), HEAD)
        for j in range(spans):
            of = pl.ds(j * lines, lines)
            key = keys[j, :, :, at].reshape(length, HEAD)
            value = values[j, :, :, at].reshape(length, HEAD)
            scores = lax.dot_general(
                query_ref[of, at], key, (((1,), (1,)), ((), ())), preferred_element_type=jnp.float32
            ) * HEAD ** (-0.5)
            live = position < lives[j] * NLEN
            masked = jnp.where(live, scores, -1e30)
            top = jnp.maximum(jnp.max(masked, axis=-1, keepdims=True), 0.0)
            probs = jnp.where(live, jnp.exp(masked - top), 0.0)
            denom = jnp.sum(probs, axis=-1, keepdims=True) + jnp.exp(-top)
            mixed = jnp.dot(probs.astype(jnp.bfloat16), value, preferred_element_type=jnp.float32)
            out_ref[of, at] = (mixed / denom).astype(out_ref.dtype)
        return carry

    lax.fori_loop(0, width // HEAD, head, 0)


def halves(first, second):
    pair = jnp.stack([first, second])
    pad = jnp.pad(pair, ((0, 0), (0, 2 * HALF - first.shape[0]), (0, 0)))
    return pad.reshape(2, 2, HALF, first.shape[1])


def call(body, ins, outs, scratch, collective_id, name):
    return pl.pallas_call(
        body,
        out_shape=outs,
        in_specs=[pl.BlockSpec(memory_space=space) for space in ins],
        out_specs=[pl.BlockSpec(memory_space=pltpu.VMEM)] * len(outs),
        scratch_shapes=scratch,
        compiler_params=pltpu.CompilerParams(collective_id=collective_id, has_side_effects=True),
        name=name,
    )


def dma(*shape):
    return pltpu.SemaphoreType.DMA(shape)


def gather_first(first, second, later, note):
    rows, width = first.shape
    zs = lax.axis_size("dp") // 2
    whole = jax.ShapeDtypeStruct((rows * zs * 2, width), first.dtype)
    outs = [
        whole,
        whole,
        jax.ShapeDtypeStruct((zs,) + later.shape[2:], later.dtype),
        jax.ShapeDtypeStruct((4,) + note.shape, note.dtype),
    ]
    one = pltpu.SemaphoreType.DMA
    scratch = [pltpu.VMEM((4, 2, zs, HALF, width), first.dtype)] + gather_sems(zs)
    scratch += [dma(2, zs // 2), dma(2, zs // 2), one, dma(3), dma(3), one]
    body = functools.partial(gather_kernel, zs)
    return call(body, [pltpu.VMEM] * 3, outs, scratch, 0, "gather_first")(halves(first, second), later, note)


def sum_over_units(parts, piece, features):
    zs = piece.shape[0]
    spans, _, rows, width = parts.shape
    whole = jax.ShapeDtypeStruct((features, piece.shape[2]), piece.dtype)
    outs = [whole, whole, jax.ShapeDtypeStruct((3, spans, rows, width), parts.dtype)]
    scratch = [pltpu.VMEM((4, 2) + piece.shape, piece.dtype), pltpu.VMEM((2, 2, rows, width), parts.dtype)]
    scratch += [dma(6), dma(6), dma(3), dma(3), dma(4), dma(4), pltpu.SemaphoreType.DMA]
    body = functools.partial(sums_kernel, zs)
    return call(body, [pltpu.VMEM] * 2, outs, scratch, 1, "sum_over_units")(piece, parts)


def route_and_attend(owners, senders, states, key, value, queries):
    spans, rows, width = states.shape
    kind = states.dtype
    outs = [jax.ShapeDtypeStruct(queries.shape, kind)]
    held = pltpu.VMEM((spans, 4, rows, key.shape[1]), kind)
    scratch = [
        pltpu.VMEM((2, rows, width), kind),
        pltpu.VMEM((10, rows, width), kind),
        pltpu.VMEM((spans, 4, rows, width), kind),
        held,
        held,
    ]
    scratch += [dma(3), dma(3), dma(6), dma(6), pltpu.SemaphoreType.DMA]
    ins = [pltpu.SMEM] * 2 + [pltpu.VMEM] * 4
    return call(route_kernel, ins, outs, scratch, 2, "route_and_attend")(owners, senders, states, key, value, queries)[0]


def on_device(neighbours, counts, owner, norm_gain, w_in, w_out, w_key, w_value, queries):
    span_count, key_len, enc_width = neighbours.shape
    m = lax.axis_index("mp")
    note = jnp.pad(jnp.stack([owner, counts]), ((0, 6), (0, 128 - span_count)))
    full_in, full_out, piece, notes = gather_first(w_in, w_out.T, halves(w_key, w_value), note)
    flat = neighbours.astype(jnp.float32).reshape(-1, enc_width)
    meansq = jnp.mean(flat * flat, axis=-1, keepdims=True)
    normed = (flat * lax.rsqrt(meansq + 1e-06) * norm_gain).astype(jnp.bfloat16)
    pre = jnp.dot(normed, full_in, preferred_element_type=jnp.float32)
    hidden = jax.nn.gelu(pre, approximate=False).astype(jnp.bfloat16)
    partial_out = jnp.dot(hidden, full_out.T, preferred_element_type=jnp.float32)
    parts = partial_out.astype(jnp.bfloat16).reshape(span_count, 4, key_len // 4, enc_width)
    full_key, full_value, got = sum_over_units(parts, piece, enc_width)
    own = lax.dynamic_index_in_dim(parts, m, 1, keepdims=False).astype(jnp.float32)
    rows = neighbours.reshape(parts.shape)
    rows = lax.dynamic_index_in_dim(rows, m, 1, keepdims=False).astype(jnp.float32)
    got = got.astype(jnp.float32)
    states = (rows + (own + got[0] + got[1] + got[2])).astype(jnp.bfloat16)
    owners = notes[:, 0, :span_count].reshape(-1)
    senders = notes[:, 1, :span_count].reshape(-1)
    return route_and_attend(owners, senders, states, full_key, full_value, queries)


def solution(mesh):
    placed = (
        P(("grp", "dp"), None, None),
        P(("grp", "dp")),
        P(("grp", "dp")),
        P(),
        P("dp", "mp"),
        P("mp", "dp"),
        P("dp", "mp"),
        P("dp", "mp"),
        P(("grp", "dp"), "mp"),
    )
    return jax.shard_map(
        on_device, mesh=mesh, in_specs=placed, out_specs=P(("grp", "dp"), "mp"), check_vma=False
    )
```

```python
import functools

import jax
import jax.numpy as jnp
from jax import lax
from jax.experimental import pallas as pl
from jax.experimental.pallas import tpu as pltpu
from jax.sharding import PartitionSpec as P

HEAD = 128
NLEN = 128
MESH = pl.DeviceIdType.MESH
HALF = 16


def ring_place():
    g, d, m = (lax.axis_index(name) for name in ("grp", "dp", "mp"))
    core, x, z = g % 2, (d % 2) * 2 + g // 2, d // 2
    return core, x, z, m


def chip_core(x, core, z, m):
    return ((x % 2) * 2 + core, z * 2 + x // 2, m)


class Gather:
    def __init__(self, zs, own_ref, out_ref, sems):
        self.zs, self.out = zs, out_ref
        (self.zsend, self.zrecv, self.fsend, self.frecv, self.one, self.psend, self.precv) = sems
        self.core, self.x, self.z, self.m = ring_place()
        turn = 1 - 2 * self.core
        self.xf, self.xb = (self.x + 4 + turn) % 4, (self.x + 4 - turn) % 4
        self.xo = (self.x + 2) % 4
        self.own = own_ref.at[self.x % 2, self.core]

    def partners(self):
        z, zs = self.z, self.zs
        return [
            chip_core(self.x, self.core, (z + 1) % zs, self.m),
            chip_core(self.x, self.core, (z + zs - 1) % zs, self.m),
            chip_core(self.xf, self.core, z, self.m),
            chip_core(self.xb, self.core, z, self.m),
            chip_core(self.x, 1 - self.core, z, self.m),
        ]

    def copy(self, src, dst, send, recv, to):
        return pltpu.make_async_remote_copy(
            src_ref=src, dst_ref=dst, send_sem=send, recv_sem=recv, device_id=to, device_id_type=MESH
        )

    def slot(self, x, z):
        return self.out.at[x, self.core, z]

    def piece(self, x):
        return self.out.at[x, self.core]

    def ring(self, plus, s):
        zs = self.zs
        at = (self.z + zs - s) % zs if plus else (self.z + s) % zs
        to = self.partners()[0 if plus else 1]
        src = self.own if s == 0 else self.slot(self.x, at)
        row = 0 if plus else 1
        return self.copy(src, self.slot(self.x, at), self.zsend.at[row, s], self.zrecv.at[row, s], to)

    def arrived(self, plus, s):
        zs = self.zs
        at = (self.z + zs - s) % zs if plus else (self.z + s) % zs
        row = 0 if plus else 1
        ref = self.slot(self.x, at)
        self.copy(ref, ref, self.zsend.at[row, s - 1], self.zrecv.at[row, s - 1], self.partners()[0]).wait_recv()

    def across(self, at, j, own):
        src = self.own if own else self.slot(self.x, at)
        dst = self.slot(self.x, at)
        to = self.partners()
        self.copy(src, dst, self.fsend, self.frecv.at[j], to[2]).start()
        self.copy(src, dst, self.one.at[0], self.one.at[1], to[3]).start()

    def relay(self, at, j):
        ref = self.slot(self.xb, at)
        self.copy(ref, ref, self.fsend, self.frecv.at[j], self.partners()[2]).wait_recv()
        self.copy(ref, ref, self.one.at[2], self.one.at[3], self.partners()[2]).start()

    def fresh(self, s):
        zs = self.zs
        if s == 0:
            return [(self.z, 0)]
        found = [((self.z + zs - s) % zs, 2 * s - 1)]
        if s <= (zs - 1) // 2:
            found.append(((self.z + s) % zs, 2 * s))
        return found

    def run(self, local, also, work):
        last, back = self.zs // 2, (self.zs - 1) // 2
        keep = pltpu.make_async_copy(self.own, self.slot(self.x, self.z), local)
        keep.start()
        for s in range(last + 1):
            if s > 0:
                self.arrived(True, s)
            if s < last:
                self.ring(True, s).start()
            if 0 < s <= back:
                self.arrived(False, s)
            if s < back:
                self.ring(False, s).start()
            also.step(s)
            for at, j in self.fresh(s):
                self.across(at, j, s == 0)
            if s < last:
                work(s)
            if s > 0:
                for at, j in self.fresh(s - 1):
                    self.relay(at, j)
        keep.wait()
        to = self.partners()[4]
        swaps = []

        def swap(x):
            ref = self.piece(x)
            i = len(swaps)
            swaps.append(self.copy(ref, ref, self.psend.at[i], self.precv.at[i], to))
            swaps[-1].start()

        swap(self.x)
        for at, j in self.fresh(last):
            self.relay(at, j)
        swap(self.xb)
        whole = self.piece(self.xf)
        self.copy(whole, whole, self.one.at[0], self.one.at[1], to).wait_recv()
        swap(self.xf)
        whole = self.piece(self.xo)
        self.copy(whole, whole, self.one.at[2], self.one.at[3], to).wait_recv()
        swap(self.xo)
        for s in range(last):
            self.ring(True, s).wait_send()
            if s < back:
                self.ring(False, s).wait_send()
        whole = self.piece(self.x)
        for sem in (self.fsend, self.one.at[0], self.one.at[2]):
            self.copy(whole, whole, sem, self.one.at[1], to).wait_send()
        for i, x in enumerate((self.x, self.xb, self.xf, self.xo)):
            swaps[i].wait_send()
            ref = self.out.at[x, 1 - self.core]
            if i in (1, 2):
                ref = self.out.at[self.xf if i == 1 else self.xb, 1 - self.core]
            self.copy(ref, ref, self.psend.at[i], self.precv.at[i], to).wait_recv()


def gather_sems(zs):
    return [
        pltpu.SemaphoreType.DMA((2, zs // 2)),
        pltpu.SemaphoreType.DMA((2, zs // 2)),
        pltpu.SemaphoreType.DMA,
        pltpu.SemaphoreType.DMA((zs,)),
        pltpu.SemaphoreType.DMA((4,)),
        pltpu.SemaphoreType.DMA((4,)),
        pltpu.SemaphoreType.DMA((4,)),
        pltpu.SemaphoreType.DMA,
    ]


def greet(partners):
    barrier = pltpu.get_barrier_semaphore()
    for to in partners:
        pl.semaphore_signal(barrier, inc=1, device_id=to, device_id_type=MESH)
    pl.semaphore_wait(barrier, len(partners))


def beside(x):
    return x + 1 - 2 * (x % 2)


class Ring(Gather):
    def __init__(self, zs, own_ref, out_ref, sems, local):
        super().__init__(zs, own_ref, out_ref, sems + (None,) * 5)
        self.local = local

    def slot(self, x, z):
        return self.out.at[z]

    def kept(self):
        return pltpu.make_async_copy(self.own, self.slot(self.x, self.z), self.local)

    def step(self, s):
        last, back = self.zs // 2, (self.zs - 1) // 2
        if s > 0:
            self.arrived(True, s)
        if s < last:
            self.ring(True, s).start()
        if 0 < s <= back:
            self.arrived(False, s)
        if s < back:
            self.ring(False, s).start()

    def finish(self):
        self.kept().wait()
        for s in range(self.zs // 2):
            self.ring(True, s).wait_send()
            if s < (self.zs - 1) // 2:
                self.ring(False, s).wait_send()


def unpad(zs, held_ref, full_refs):
    rows = full_refs[0].shape[0] // (2 * zs)
    for a, full in enumerate(full_refs):
        for z in range(zs):
            for high in range(2):
                at = (2 * z + high) * rows
                full[at : at + HALF] = held_ref[high * 2 + a, 0, z]
                full[at + HALF : at + rows] = held_ref[high * 2 + a, 1, z, : rows - HALF]


def normalise(steps, token_ref, gain_ref, normed_ref, s):
    spans, quarters = token_ref.shape[:2]
    share = spans * quarters // steps
    for q in range(s * share, (s + 1) * share):
        block = token_ref[q // quarters, q % quarters].astype(jnp.float32)
        meansq = jnp.mean(block * block, axis=-1, keepdims=True)
        made = block * lax.rsqrt(meansq + 1e-06) * gain_ref[...]
        normed_ref[q // quarters, q % quarters] = made.astype(normed_ref.dtype)


def gather_kernel(zs, own_ref, later_ref, note_ref, token_ref, gain_ref, in_ref, out_ref, piece_ref, notes_ref, normed_ref, held, *sems):
    moves = Gather(zs, own_ref, held, sems[:7])
    also = Ring(zs, later_ref, piece_ref, sems[8:10], sems[10])
    nsend, nrecv, nlocal = sems[11:]
    core, x, z, m = ring_place()
    near = [
        chip_core(x, 1 - core, z, m),
        chip_core(beside(x), core, z, m),
        chip_core(beside(x), 1 - core, z, m),
    ]
    g = lax.axis_index("grp")
    greet(moves.partners() + near[2:])
    keep = pltpu.make_async_copy(note_ref, notes_ref.at[g], nlocal)
    keep.start()
    also.kept().start()
    told = []
    for i, to in enumerate(near):
        told.append(moves.copy(note_ref, notes_ref.at[g], nsend.at[i], nrecv.at[i], to))
        told[-1].start()
    moves.run(sems[7], also, functools.partial(normalise, zs // 2, token_ref, gain_ref, normed_ref))
    unpad(zs, held, (in_ref, out_ref))
    also.finish()
    keep.wait()
    for i, copy in enumerate(told):
        copy.wait_send()
        from_core = core if i == 1 else 1 - core
        from_low = x % 2 if i == 0 else 1 - x % 2
        ref = notes_ref.at[from_low * 2 + from_core]
        moves.copy(ref, ref, nsend.at[i], nrecv.at[i], near[i]).wait_recv()


def remote(src, dst, sends, recvs, i, to):
    return pltpu.make_async_remote_copy(
        src_ref=src, dst_ref=dst, send_sem=sends.at[i], recv_sem=recvs.at[i], device_id=to, device_id_type=MESH
    )


def encode(normed_ref, in_ref, out_ref, of):
    spans, _, rows, width = normed_ref.shape
    block = normed_ref[:, of].reshape(spans * rows, width)
    pre = jnp.dot(block, in_ref[...], preferred_element_type=jnp.float32)
    hidden = (0.5 * pre * (1.0 + lax.erf(pre * 0.5**0.5))).astype(block.dtype)
    made = lax.dot_general(hidden, out_ref[...], (((1,), (1,)), ((), ())), preferred_element_type=jnp.float32)
    return made.reshape(spans, rows, width)


def sums_kernel(zs, piece_ref, normed_ref, token_ref, in_ref, out_ref, key_ref, value_ref, states_ref, held, part_ref, own_ref, got_ref, relay, ysend, yrecv, xsend, xrecv, psend, precv, local):
    core, x, z, m = ring_place()
    turn = 1 - 2 * core
    xf, xb, xo = (x + 4 + turn) % 4, (x + 4 - turn) % 4, (x + 2) % 4
    up, down, far = (m + 1) % 4, (m + 3) % 4, (m + 2) % 4
    to_up, to_down = chip_core(x, core, z, up), chip_core(x, core, z, down)
    to_f, to_b = chip_core(xf, core, z, m), chip_core(xb, core, z, m)
    to_core = chip_core(x, 1 - core, z, m)
    greet([to_f, to_b, to_core, to_up, to_down])

    def make(i, src, dst, to):
        return remote(src, dst, ysend, yrecv, i, to)

    low, high = pl.ds(0, 2), pl.ds(2, 2)
    copies = [
        make(0, part_ref.at[low, far], relay.at[0], to_up),
        make(1, part_ref.at[high, far], relay.at[1], to_down),
        make(2, part_ref.at[:, up], got_ref.at[0], to_up),
        make(3, part_ref.at[:, down], got_ref.at[1], to_down),
        make(4, relay.at[0], got_ref.at[2, low], to_up),
        make(5, relay.at[1], got_ref.at[2, high], to_down),
    ]
    keep = pltpu.make_async_copy(piece_ref, held.at[x, core], local)
    keep.start()
    here = held.at[x, core]
    back, front, over = held.at[xb, core], held.at[xf, core], held.at[xo, core]
    to_front = remote(piece_ref, here, xsend, xrecv, 0, to_f)
    to_back = remote(piece_ref, here, xsend, xrecv, 1, to_b)
    onward = remote(back, back, xsend, xrecv, 2, to_f)
    to_front.start()
    to_back.start()
    swaps = [remote(ref, ref, psend, precv, i, to_core) for i, ref in enumerate((here, back, front, over))]
    for of, ready in ((far, copies[:2]), (up, copies[2:3]), (down, copies[3:4])):
        part_ref[:, of] = encode(normed_ref, in_ref, out_ref, of).astype(part_ref.dtype)
        for copy in ready:
            copy.start()
    keep.wait()
    swaps[0].start()
    for i in range(2):
        copies[i].wait_recv()
        copies[4 + i].start()
    remote(back, back, xsend, xrecv, 0, to_f).wait_recv()
    onward.start()
    swaps[1].start()
    own_ref[...] = encode(normed_ref, in_ref, out_ref, m)
    remote(front, front, xsend, xrecv, 1, to_b).wait_recv()
    swaps[2].start()
    remote(over, over, xsend, xrecv, 2, to_f).wait_recv()
    swaps[3].start()
    for i, at in enumerate((x, xf, xb, xo)):
        ref = held.at[at, 1 - core]
        remote(ref, ref, psend, precv, i, to_core).wait_recv()
    unpad(zs, held, (key_ref, value_ref))
    for copy in copies[2:]:
        copy.wait_recv()
    for j in range(states_ref.shape[0]):
        total = own_ref[j]
        for i in range(3):
            total += got_ref[i, j].astype(jnp.float32)
        states_ref[j] = (token_ref[j, m].astype(jnp.float32) + total).astype(states_ref.dtype)
    for copy in copies + [to_front, to_back, onward] + swaps:
        copy.wait_send()


def route_kernel(note_ref, states_ref, key_ref, value_ref, query_ref, out_ref, send, cand, full_ref, keys, values, rsend, rrecv, ysend, yrecv, local):
    core, x, z, m = ring_place()
    g, d = lax.axis_index("grp"), lax.axis_index("dp")
    up, down, far = (m + 1) % 4, (m + 3) % 4, (m + 2) % 4
    to_up, to_down = chip_core(x, core, z, up), chip_core(x, core, z, down)
    to_core, to_side = chip_core(x, 1 - core, z, m), chip_core(beside(x), core, z, m)
    spans, block = 4, 4 * lax.axis_size("dp")

    picks = [jnp.int32(0)] * 2
    finds = [jnp.int32(0)] * spans
    lives = [jnp.int32(0)] * spans
    for source in range(4):
        low_gap = jnp.where(g // 2 == source // 2, 0, 2)
        apart = low_gap + jnp.where(core == source % 2, 0, 1)
        rank = jnp.int32(0)
        for i in range(spans):
            target = note_ref[source, 0, i]
            leaves = (target < source * block) | (target >= (source + 1) * block)
            for r in range(2):
                picks[r] = jnp.where(leaves & (rank == r) & (apart == 0), i, picks[r])
            spot = jnp.where(apart == 0, i, 4 + 2 * (apart - 1) + jnp.minimum(rank, 1))
            for j in range(spans):
                mine = target == (g * lax.axis_size("dp") + d) * spans + j
                finds[j] = jnp.where(mine, spot, finds[j])
                lives[j] = jnp.where(mine, note_ref[source, 1, i], lives[j])
            rank = rank + jnp.where(leaves, 1, 0)

    for r in range(2):
        send[r] = states_ref[picks[r]]
    greet([to_core, to_side, to_up, to_down])
    first = [
        remote(send, cand.at[pl.ds(4, 2)], rsend, rrecv, 0, to_core),
        remote(send, cand.at[pl.ds(6, 2)], rsend, rrecv, 1, to_side),
        remote(cand.at[pl.ds(6, 2)], cand.at[pl.ds(8, 2)], rsend, rrecv, 2, to_core),
    ]
    first[1].start()
    first[0].start()
    held = pltpu.make_async_copy(states_ref, cand.at[pl.ds(0, 4)], local)
    held.start()
    first[1].wait_recv()
    first[2].start()
    first[0].wait_recv()
    held.wait()
    first[2].wait_recv()
    for j in range(spans):
        full_ref[j, m] = cand[finds[j]]

    low, high = pl.ds(0, 2), pl.ds(2, 2)

    def share(i, rows, of, to):
        ref = full_ref.at[rows, of]
        return remote(ref, ref, ysend, yrecv, i, to)

    shares = [
        share(0, low, m, to_up),
        share(1, high, m, to_down),
        share(2, high, m, to_up),
        share(3, low, m, to_down),
        share(4, low, down, to_up),
        share(5, high, up, to_down),
    ]
    arrivals = [
        share(0, low, down, to_up),
        share(1, high, up, to_down),
        share(2, high, down, to_up),
        share(3, low, up, to_down),
        share(4, low, far, to_up),
        share(5, high, far, to_down),
    ]
    for one in shares[:4]:
        one.start()
    project = functools.partial(project_rows, full_ref, ((key_ref, keys), (value_ref, values)))
    for i in range(2):
        arrivals[i].wait_recv()
        shares[4 + i].start()
    project(m)
    arrivals[2].wait_recv()
    project(down)
    arrivals[3].wait_recv()
    project(up)
    arrivals[4].wait_recv()
    arrivals[5].wait_recv()
    project(far)
    attend(query_ref, keys, values, lives, out_ref)
    for one in shares + first:
        one.wait_send()


def project_rows(full_ref, pairs, of):
    spans, _, rows, width = full_ref.shape
    block = full_ref[:, of].reshape(spans * rows, width)
    tile = min(256, pairs[0][0].shape[1])
    for weight, result in pairs:

        def column(t, carry, weight=weight, result=result):
            at = pl.ds(pl.multiple_of(t * tile, tile), tile)
            made = jnp.dot(block, weight[:, at], preferred_element_type=jnp.float32)
            result[:, of, :, at] = made.astype(result.dtype).reshape(spans, rows, tile)
            return carry

        lax.fori_loop(0, weight.shape[1] // tile, column, 0)


def attend(query_ref, keys, values, lives, out_ref):
    spans, quarters, rows, width = keys.shape
    length = quarters * rows
    lines = query_ref.shape[0] // spans
    position = lax.broadcasted_iota(jnp.int32, (lines, length), 1)

    def head(h, carry):
        at = pl.ds(pl.multiple_of(h * HEAD, HEAD), HEAD)
        for j in range(spans):
            of = pl.ds(j * lines, lines)
            key = keys[j, :, :, at].reshape(length, HEAD)
            value = values[j, :, :, at].reshape(length, HEAD)
            scores = lax.dot_general(
                query_ref[of, at], key, (((1,), (1,)), ((), ())), preferred_element_type=jnp.float32
            ) * HEAD ** (-0.5)
            live = position < lives[j] * NLEN
            masked = jnp.where(live, scores, -1e30)
            top = jnp.maximum(jnp.max(masked, axis=-1, keepdims=True), 0.0)
            probs = jnp.where(live, jnp.exp(masked - top), 0.0)
            denom = jnp.sum(probs, axis=-1, keepdims=True) + jnp.exp(-top)
            mixed = jnp.dot(probs.astype(jnp.bfloat16), value, preferred_element_type=jnp.float32)
            out_ref[of, at] = (mixed / denom).astype(out_ref.dtype)
        return carry

    lax.fori_loop(0, width // HEAD, head, 0)


def halves(first, second):
    pair = jnp.stack([first, second])
    pad = jnp.pad(pair, ((0, 0), (0, 2 * HALF - first.shape[0]), (0, 0)))
    return pad.reshape(2, 2, HALF, first.shape[1])


def call(body, ins, outs, scratch, collective_id, name):
    return pl.pallas_call(
        body,
        out_shape=outs,
        in_specs=[pl.BlockSpec(memory_space=space) for space in ins],
        out_specs=[pl.BlockSpec(memory_space=pltpu.VMEM)] * len(outs),
        scratch_shapes=scratch,
        compiler_params=pltpu.CompilerParams(collective_id=collective_id, has_side_effects=True),
        name=name,
    )


def dma(*shape):
    return pltpu.SemaphoreType.DMA(shape)


def gather_first(first, second, later, note, tokens, gain):
    rows, width = first.shape
    zs = lax.axis_size("dp") // 2
    whole = jax.ShapeDtypeStruct((rows * zs * 2, width), first.dtype)
    outs = [
        whole,
        whole,
        jax.ShapeDtypeStruct((zs,) + later.shape[2:], later.dtype),
        jax.ShapeDtypeStruct((4,) + note.shape, note.dtype),
        jax.ShapeDtypeStruct(tokens.shape, tokens.dtype),
    ]
    one = pltpu.SemaphoreType.DMA
    scratch = [pltpu.VMEM((4, 2, zs, HALF, width), first.dtype)] + gather_sems(zs)
    scratch += [dma(2, zs // 2), dma(2, zs // 2), one, dma(3), dma(3), one]
    body = functools.partial(gather_kernel, zs)
    ins = (halves(first, second), later, note, tokens, gain)
    return call(body, [pltpu.VMEM] * 5, outs, scratch, 0, "gather_first")(*ins)


def encode_and_sum(piece, normed, tokens, full_in, full_out):
    zs = piece.shape[0]
    spans, _, rows, width = tokens.shape
    kind = tokens.dtype
    whole = jax.ShapeDtypeStruct((width, piece.shape[2]), kind)
    outs = [whole, whole, jax.ShapeDtypeStruct((spans, rows, width), kind)]
    scratch = [
        pltpu.VMEM((4, 2) + piece.shape, kind),
        pltpu.VMEM(tokens.shape, kind),
        pltpu.VMEM((spans, rows, width), jnp.float32),
        pltpu.VMEM((3, spans, rows, width), kind),
        pltpu.VMEM((2, 2, rows, width), kind),
    ]
    scratch += [dma(6), dma(6), dma(3), dma(3), dma(4), dma(4), pltpu.SemaphoreType.DMA]
    body = functools.partial(sums_kernel, zs)
    ins = (piece, normed, tokens, full_in, full_out)
    return call(body, [pltpu.VMEM] * 5, outs, scratch, 1, "encode_and_sum")(*ins)


def route_and_attend(notes, states, key, value, queries):
    spans, rows, width = states.shape
    kind = states.dtype
    outs = [jax.ShapeDtypeStruct(queries.shape, kind)]
    held = pltpu.VMEM((spans, 4, rows, key.shape[1]), kind)
    scratch = [
        pltpu.VMEM((2, rows, width), kind),
        pltpu.VMEM((10, rows, width), kind),
        pltpu.VMEM((spans, 4, rows, width), kind),
        held,
        held,
    ]
    scratch += [dma(3), dma(3), dma(6), dma(6), pltpu.SemaphoreType.DMA]
    ins = [pltpu.SMEM] + [pltpu.VMEM] * 4
    return call(route_kernel, ins, outs, scratch, 2, "route_and_attend")(notes, states, key, value, queries)[0]


def on_device(neighbours, counts, owner, norm_gain, w_in, w_out, w_key, w_value, queries):
    span_count, key_len, enc_width = neighbours.shape
    tokens = neighbours.reshape(span_count, 4, key_len // 4, enc_width)
    note = jnp.pad(jnp.stack([owner, counts]), ((0, 6), (0, 128 - span_count)))
    later = halves(w_key, w_value)
    gain = norm_gain.reshape(1, enc_width)
    full_in, full_out, piece, notes, normed = gather_first(w_in, w_out.T, later, note, tokens, gain)
    full_key, full_value, states = encode_and_sum(piece, normed, tokens, full_in, full_out)
    return route_and_attend(notes, states, full_key, full_value, queries)


def solution(mesh):
    placed = (
        P(("grp", "dp"), None, None),
        P(("grp", "dp")),
        P(("grp", "dp")),
        P(),
        P("dp", "mp"),
        P("mp", "dp"),
        P("dp", "mp"),
        P("dp", "mp"),
        P(("grp", "dp"), "mp"),
    )
    return jax.shard_map(
        on_device, mesh=mesh, in_specs=placed, out_specs=P(("grp", "dp"), "mp"), check_vma=False
    )
```

```python
import functools

import jax
import jax.numpy as jnp
from jax import lax
from jax.experimental import pallas as pl
from jax.experimental.pallas import tpu as pltpu
from jax.sharding import PartitionSpec as P

HEAD = 128
NLEN = 128
MESH = pl.DeviceIdType.MESH
HALF = 16


def ring_place():
    g, d, m = (lax.axis_index(name) for name in ("grp", "dp", "mp"))
    core, x, z = g % 2, (d % 2) * 2 + g // 2, d // 2
    return core, x, z, m


def chip_core(x, core, z, m):
    return ((x % 2) * 2 + core, z * 2 + x // 2, m)


class Gather:
    def __init__(self, zs, own_ref, out_ref, sems):
        self.zs, self.out = zs, out_ref
        (self.zsend, self.zrecv, self.fsend, self.frecv, self.one, self.psend, self.precv) = sems
        self.core, self.x, self.z, self.m = ring_place()
        turn = 1 - 2 * self.core
        self.xf, self.xb = (self.x + 4 + turn) % 4, (self.x + 4 - turn) % 4
        self.xo = (self.x + 2) % 4
        self.own = own_ref.at[self.x % 2, self.core]

    def partners(self):
        z, zs = self.z, self.zs
        return [
            chip_core(self.x, self.core, (z + 1) % zs, self.m),
            chip_core(self.x, self.core, (z + zs - 1) % zs, self.m),
            chip_core(self.xf, self.core, z, self.m),
            chip_core(self.xb, self.core, z, self.m),
            chip_core(self.x, 1 - self.core, z, self.m),
        ]

    def copy(self, src, dst, send, recv, to):
        return pltpu.make_async_remote_copy(
            src_ref=src, dst_ref=dst, send_sem=send, recv_sem=recv, device_id=to, device_id_type=MESH
        )

    def slot(self, x, z):
        return self.out.at[x, self.core, z]

    def piece(self, x):
        return self.out.at[x, self.core]

    def ring(self, plus, s):
        zs = self.zs
        at = (self.z + zs - s) % zs if plus else (self.z + s) % zs
        to = self.partners()[0 if plus else 1]
        src = self.own if s == 0 else self.slot(self.x, at)
        row = 0 if plus else 1
        return self.copy(src, self.slot(self.x, at), self.zsend.at[row, s], self.zrecv.at[row, s], to)

    def arrived(self, plus, s):
        zs = self.zs
        at = (self.z + zs - s) % zs if plus else (self.z + s) % zs
        row = 0 if plus else 1
        ref = self.slot(self.x, at)
        self.copy(ref, ref, self.zsend.at[row, s - 1], self.zrecv.at[row, s - 1], self.partners()[0]).wait_recv()

    def across(self, at, j, own):
        src = self.own if own else self.slot(self.x, at)
        dst = self.slot(self.x, at)
        to = self.partners()
        self.copy(src, dst, self.fsend, self.frecv.at[j], to[2]).start()
        self.copy(src, dst, self.one.at[0], self.one.at[1], to[3]).start()

    def relay(self, at, j):
        ref = self.slot(self.xb, at)
        self.copy(ref, ref, self.fsend, self.frecv.at[j], self.partners()[2]).wait_recv()
        self.copy(ref, ref, self.one.at[2], self.one.at[3], self.partners()[2]).start()

    def fresh(self, s):
        zs = self.zs
        if s == 0:
            return [(self.z, 0)]
        found = [((self.z + zs - s) % zs, 2 * s - 1)]
        if s <= (zs - 1) // 2:
            found.append(((self.z + s) % zs, 2 * s))
        return found

    def run(self, local, also, work):
        last, back = self.zs // 2, (self.zs - 1) // 2
        keep = pltpu.make_async_copy(self.own, self.slot(self.x, self.z), local)
        keep.start()
        for s in range(last + 1):
            if s > 0:
                self.arrived(True, s)
            if s < last:
                self.ring(True, s).start()
            if 0 < s <= back:
                self.arrived(False, s)
            if s < back:
                self.ring(False, s).start()
            also.step(s)
            for at, j in self.fresh(s):
                self.across(at, j, s == 0)
            if s < last:
                work(s)
            if s > 0:
                for at, j in self.fresh(s - 1):
                    self.relay(at, j)
        keep.wait()
        to = self.partners()[4]
        swaps = []

        def swap(x):
            ref = self.piece(x)
            i = len(swaps)
            swaps.append(self.copy(ref, ref, self.psend.at[i], self.precv.at[i], to))
            swaps[-1].start()

        swap(self.x)
        for at, j in self.fresh(last):
            self.relay(at, j)
        swap(self.xb)
        whole = self.piece(self.xf)
        self.copy(whole, whole, self.one.at[0], self.one.at[1], to).wait_recv()
        swap(self.xf)
        whole = self.piece(self.xo)
        self.copy(whole, whole, self.one.at[2], self.one.at[3], to).wait_recv()
        swap(self.xo)
        for s in range(last):
            self.ring(True, s).wait_send()
            if s < back:
                self.ring(False, s).wait_send()
        whole = self.piece(self.x)
        for sem in (self.fsend, self.one.at[0], self.one.at[2]):
            self.copy(whole, whole, sem, self.one.at[1], to).wait_send()
        for i, x in enumerate((self.x, self.xb, self.xf, self.xo)):
            swaps[i].wait_send()
            ref = self.out.at[x, 1 - self.core]
            if i in (1, 2):
                ref = self.out.at[self.xf if i == 1 else self.xb, 1 - self.core]
            self.copy(ref, ref, self.psend.at[i], self.precv.at[i], to).wait_recv()


def gather_sems(zs):
    return [
        pltpu.SemaphoreType.DMA((2, zs // 2)),
        pltpu.SemaphoreType.DMA((2, zs // 2)),
        pltpu.SemaphoreType.DMA,
        pltpu.SemaphoreType.DMA((zs,)),
        pltpu.SemaphoreType.DMA((4,)),
        pltpu.SemaphoreType.DMA((4,)),
        pltpu.SemaphoreType.DMA((4,)),
        pltpu.SemaphoreType.DMA,
    ]


def greet(partners):
    barrier = pltpu.get_barrier_semaphore()
    for to in partners:
        pl.semaphore_signal(barrier, inc=1, device_id=to, device_id_type=MESH)
    pl.semaphore_wait(barrier, len(partners))


def beside(x):
    return x + 1 - 2 * (x % 2)


class Ring(Gather):
    def __init__(self, zs, own_ref, out_ref, sems, local):
        super().__init__(zs, own_ref, out_ref, sems + (None,) * 5)
        self.local = local

    def slot(self, x, z):
        return self.out.at[z]

    def kept(self):
        return pltpu.make_async_copy(self.own, self.slot(self.x, self.z), self.local)

    def step(self, s):
        last, back = self.zs // 2, (self.zs - 1) // 2
        if s > 0:
            self.arrived(True, s)
        if s < last:
            self.ring(True, s).start()
        if 0 < s <= back:
            self.arrived(False, s)
        if s < back:
            self.ring(False, s).start()

    def finish(self):
        self.kept().wait()
        for s in range(self.zs // 2):
            self.ring(True, s).wait_send()
            if s < (self.zs - 1) // 2:
                self.ring(False, s).wait_send()


def unpad(zs, held_ref, full_refs):
    rows = full_refs[0].shape[0] // (2 * zs)
    for a, full in enumerate(full_refs):
        for z in range(zs):
            for high in range(2):
                at = (2 * z + high) * rows
                full[at : at + HALF] = held_ref[high * 2 + a, 0, z]
                full[at + HALF : at + rows] = held_ref[high * 2 + a, 1, z, : rows - HALF]


def normalise(steps, token_ref, gain_ref, normed_ref, s):
    spans, quarters = token_ref.shape[:2]
    share = spans * quarters // steps
    for q in range(s * share, (s + 1) * share):
        block = token_ref[q // quarters, q % quarters].astype(jnp.float32)
        meansq = jnp.mean(block * block, axis=-1, keepdims=True)
        made = block * lax.rsqrt(meansq + 1e-06) * gain_ref[...].reshape(1, -1)
        normed_ref[q // quarters, q % quarters] = made.astype(normed_ref.dtype)


def lay_out(half_ref, weights):
    for a, weight in enumerate(weights):
        rest = weight.shape[0] - HALF
        half_ref[a, 0] = weight[:HALF]
        half_ref[a, 1, :rest] = weight[HALF:]
        half_ref[a, 1, rest:] = jnp.zeros((HALF - rest, weight.shape[1]), weight.dtype)


def write_note(note_ref, lists):
    row = lax.broadcasted_iota(jnp.int32, note_ref.shape, 0)
    lane = lax.broadcasted_iota(jnp.int32, note_ref.shape, 1)
    made = jnp.zeros(note_ref.shape, jnp.int32)
    for k, values in enumerate(lists):
        for i in range(values.shape[0]):
            made = jnp.where((row == k) & (lane == i), values[i], made)
    note_ref[...] = made


def gather_kernel(zs, owner_ref, count_ref, win_ref, wout_ref, wkey_ref, wvalue_ref, token_ref, gain_ref, in_ref, out_ref, piece_ref, notes_ref, normed_ref, held, own_ref, later_ref, note_ref, *sems):
    lay_out(own_ref, (win_ref, wout_ref))
    lay_out(later_ref, (wkey_ref, wvalue_ref))
    write_note(note_ref, (owner_ref, count_ref))
    moves = Gather(zs, own_ref, held, sems[:7])
    also = Ring(zs, later_ref, piece_ref, sems[8:10], sems[10])
    nsend, nrecv, nlocal = sems[11:]
    core, x, z, m = ring_place()
    near = [
        chip_core(x, 1 - core, z, m),
        chip_core(beside(x), core, z, m),
        chip_core(beside(x), 1 - core, z, m),
    ]
    g = lax.axis_index("grp")
    greet(moves.partners() + near[2:])
    keep = pltpu.make_async_copy(note_ref, notes_ref.at[g], nlocal)
    keep.start()
    also.kept().start()
    told = []
    for i, to in enumerate(near):
        told.append(moves.copy(note_ref, notes_ref.at[g], nsend.at[i], nrecv.at[i], to))
        told[-1].start()
    moves.run(sems[7], also, functools.partial(normalise, zs // 2, token_ref, gain_ref, normed_ref))
    unpad(zs, held, (in_ref, out_ref))
    also.finish()
    keep.wait()
    for i, copy in enumerate(told):
        copy.wait_send()
        from_core = core if i == 1 else 1 - core
        from_low = x % 2 if i == 0 else 1 - x % 2
        ref = notes_ref.at[from_low * 2 + from_core]
        moves.copy(ref, ref, nsend.at[i], nrecv.at[i], near[i]).wait_recv()


def remote(src, dst, sends, recvs, i, to):
    return pltpu.make_async_remote_copy(
        src_ref=src, dst_ref=dst, send_sem=sends.at[i], recv_sem=recvs.at[i], device_id=to, device_id_type=MESH
    )


def encode(normed_ref, in_ref, out_ref, of):
    spans, _, rows, width = normed_ref.shape
    block = normed_ref[:, of].reshape(spans * rows, width)
    pre = jnp.dot(block, in_ref[...], preferred_element_type=jnp.float32)
    hidden = (0.5 * pre * (1.0 + lax.erf(pre * 0.5**0.5))).astype(block.dtype)
    made = lax.dot_general(hidden, out_ref[...], (((1,), (1,)), ((), ())), preferred_element_type=jnp.float32)
    return made.reshape(spans, rows, width)


def sums_kernel(zs, piece_ref, normed_ref, token_ref, in_ref, out_ref, key_ref, value_ref, states_ref, held, part_ref, own_ref, got_ref, relay, ysend, yrecv, xsend, xrecv, psend, precv, local):
    core, x, z, m = ring_place()
    turn = 1 - 2 * core
    xf, xb, xo = (x + 4 + turn) % 4, (x + 4 - turn) % 4, (x + 2) % 4
    up, down, far = (m + 1) % 4, (m + 3) % 4, (m + 2) % 4
    to_up, to_down = chip_core(x, core, z, up), chip_core(x, core, z, down)
    to_f, to_b = chip_core(xf, core, z, m), chip_core(xb, core, z, m)
    to_core = chip_core(x, 1 - core, z, m)
    greet([to_f, to_b, to_core, to_up, to_down])

    def make(i, src, dst, to):
        return remote(src, dst, ysend, yrecv, i, to)

    low, high = pl.ds(0, 2), pl.ds(2, 2)
    copies = [
        make(0, part_ref.at[low, far], relay.at[0], to_up),
        make(1, part_ref.at[high, far], relay.at[1], to_down),
        make(2, part_ref.at[:, up], got_ref.at[0], to_up),
        make(3, part_ref.at[:, down], got_ref.at[1], to_down),
        make(4, relay.at[0], got_ref.at[2, low], to_up),
        make(5, relay.at[1], got_ref.at[2, high], to_down),
    ]
    keep = pltpu.make_async_copy(piece_ref, held.at[x, core], local)
    keep.start()
    here = held.at[x, core]
    back, front, over = held.at[xb, core], held.at[xf, core], held.at[xo, core]
    to_front = remote(piece_ref, here, xsend, xrecv, 0, to_f)
    to_back = remote(piece_ref, here, xsend, xrecv, 1, to_b)
    onward = remote(back, back, xsend, xrecv, 2, to_f)
    to_front.start()
    to_back.start()
    swaps = [remote(ref, ref, psend, precv, i, to_core) for i, ref in enumerate((here, back, front, over))]
    for of, ready in ((far, copies[:2]), (up, copies[2:3]), (down, copies[3:4])):
        part_ref[:, of] = encode(normed_ref, in_ref, out_ref, of).astype(part_ref.dtype)
        for copy in ready:
            copy.start()
    keep.wait()
    swaps[0].start()
    for i in range(2):
        copies[i].wait_recv()
        copies[4 + i].start()
    remote(back, back, xsend, xrecv, 0, to_f).wait_recv()
    onward.start()
    swaps[1].start()
    own_ref[...] = encode(normed_ref, in_ref, out_ref, m)
    remote(front, front, xsend, xrecv, 1, to_b).wait_recv()
    swaps[2].start()
    remote(over, over, xsend, xrecv, 2, to_f).wait_recv()
    swaps[3].start()
    for i, at in enumerate((x, xf, xb, xo)):
        ref = held.at[at, 1 - core]
        remote(ref, ref, psend, precv, i, to_core).wait_recv()
    unpad(zs, held, (key_ref, value_ref))
    for copy in copies[2:]:
        copy.wait_recv()
    for j in range(states_ref.shape[0]):
        total = own_ref[j]
        for i in range(3):
            total += got_ref[i, j].astype(jnp.float32)
        states_ref[j] = (token_ref[j, m].astype(jnp.float32) + total).astype(states_ref.dtype)
    for copy in copies + [to_front, to_back, onward] + swaps:
        copy.wait_send()


def route_kernel(note_ref, states_ref, key_ref, value_ref, query_ref, out_ref, send, cand, full_ref, keys, values, rsend, rrecv, ysend, yrecv, local):
    core, x, z, m = ring_place()
    g, d = lax.axis_index("grp"), lax.axis_index("dp")
    up, down, far = (m + 1) % 4, (m + 3) % 4, (m + 2) % 4
    to_up, to_down = chip_core(x, core, z, up), chip_core(x, core, z, down)
    to_core, to_side = chip_core(x, 1 - core, z, m), chip_core(beside(x), core, z, m)
    spans, block = 4, 4 * lax.axis_size("dp")

    picks = [jnp.int32(0)] * 2
    finds = [jnp.int32(0)] * spans
    lives = [jnp.int32(0)] * spans
    for source in range(4):
        low_gap = jnp.where(g // 2 == source // 2, 0, 2)
        apart = low_gap + jnp.where(core == source % 2, 0, 1)
        rank = jnp.int32(0)
        for i in range(spans):
            target = note_ref[source, 0, i]
            leaves = (target < source * block) | (target >= (source + 1) * block)
            for r in range(2):
                picks[r] = jnp.where(leaves & (rank == r) & (apart == 0), i, picks[r])
            spot = jnp.where(apart == 0, i, 4 + 2 * (apart - 1) + jnp.minimum(rank, 1))
            for j in range(spans):
                mine = target == (g * lax.axis_size("dp") + d) * spans + j
                finds[j] = jnp.where(mine, spot, finds[j])
                lives[j] = jnp.where(mine, note_ref[source, 1, i], lives[j])
            rank = rank + jnp.where(leaves, 1, 0)

    for r in range(2):
        send[r] = states_ref[picks[r]]
    greet([to_core, to_side, to_up, to_down])
    first = [
        remote(send, cand.at[pl.ds(4, 2)], rsend, rrecv, 0, to_core),
        remote(send, cand.at[pl.ds(6, 2)], rsend, rrecv, 1, to_side),
        remote(cand.at[pl.ds(6, 2)], cand.at[pl.ds(8, 2)], rsend, rrecv, 2, to_core),
    ]
    first[1].start()
    first[0].start()
    held = pltpu.make_async_copy(states_ref, cand.at[pl.ds(0, 4)], local)
    held.start()
    first[1].wait_recv()
    first[2].start()
    first[0].wait_recv()
    held.wait()
    first[2].wait_recv()
    for j in range(spans):
        full_ref[j, m] = cand[finds[j]]

    low, high = pl.ds(0, 2), pl.ds(2, 2)

    def share(i, rows, of, to):
        ref = full_ref.at[rows, of]
        return remote(ref, ref, ysend, yrecv, i, to)

    shares = [
        share(0, low, m, to_up),
        share(1, high, m, to_down),
        share(2, high, m, to_up),
        share(3, low, m, to_down),
        share(4, low, down, to_up),
        share(5, high, up, to_down),
    ]
    arrivals = [
        share(0, low, down, to_up),
        share(1, high, up, to_down),
        share(2, high, down, to_up),
        share(3, low, up, to_down),
        share(4, low, far, to_up),
        share(5, high, far, to_down),
    ]
    for one in shares[:4]:
        one.start()
    project = functools.partial(project_rows, full_ref, ((key_ref, keys), (value_ref, values)))
    for i in range(2):
        arrivals[i].wait_recv()
        shares[4 + i].start()
    project(m)
    arrivals[2].wait_recv()
    project(down)
    arrivals[3].wait_recv()
    project(up)
    arrivals[4].wait_recv()
    arrivals[5].wait_recv()
    project(far)
    attend(query_ref, keys, values, lives, out_ref)
    for one in shares + first:
        one.wait_send()


def project_rows(full_ref, pairs, of):
    spans, _, rows, width = full_ref.shape
    block = full_ref[:, of].reshape(spans * rows, width)
    tile = min(256, pairs[0][0].shape[1])
    for weight, result in pairs:

        def column(t, carry, weight=weight, result=result):
            at = pl.ds(pl.multiple_of(t * tile, tile), tile)
            made = jnp.dot(block, weight[:, at], preferred_element_type=jnp.float32)
            result[:, of, :, at] = made.astype(result.dtype).reshape(spans, rows, tile)
            return carry

        lax.fori_loop(0, weight.shape[1] // tile, column, 0)


def attend(query_ref, keys, values, lives, out_ref):
    spans, quarters, rows, width = keys.shape
    length = quarters * rows
    lines = query_ref.shape[0] // spans
    position = lax.broadcasted_iota(jnp.int32, (lines, length), 1)

    def head(h, carry):
        at = pl.ds(pl.multiple_of(h * HEAD, HEAD), HEAD)
        for j in range(spans):
            of = pl.ds(j * lines, lines)
            key = keys[j, :, :, at].reshape(length, HEAD)
            value = values[j, :, :, at].reshape(length, HEAD)
            scores = lax.dot_general(
                query_ref[of, at], key, (((1,), (1,)), ((), ())), preferred_element_type=jnp.float32
            ) * HEAD ** (-0.5)
            live = position < lives[j] * NLEN
            masked = jnp.where(live, scores, -1e30)
            top = jnp.maximum(jnp.max(masked, axis=-1, keepdims=True), 0.0)
            probs = jnp.where(live, jnp.exp(masked - top), 0.0)
            denom = jnp.sum(probs, axis=-1, keepdims=True) + jnp.exp(-top)
            mixed = jnp.dot(probs.astype(jnp.bfloat16), value, preferred_element_type=jnp.float32)
            out_ref[of, at] = (mixed / denom).astype(out_ref.dtype)
        return carry

    lax.fori_loop(0, width // HEAD, head, 0)


def call(body, ins, outs, scratch, collective_id, name):
    return pl.pallas_call(
        body,
        out_shape=outs,
        in_specs=[pl.BlockSpec(memory_space=space) for space in ins],
        out_specs=[pl.BlockSpec(memory_space=pltpu.VMEM)] * len(outs),
        scratch_shapes=scratch,
        compiler_params=pltpu.CompilerParams(collective_id=collective_id, has_side_effects=True),
        name=name,
    )


def dma(*shape):
    return pltpu.SemaphoreType.DMA(shape)


def gather_first(owner, counts, first, second, key, value, tokens, gain):
    rows, width = first.shape
    zs = lax.axis_size("dp") // 2
    kind = first.dtype
    whole = jax.ShapeDtypeStruct((rows * zs * 2, width), kind)
    outs = [
        whole,
        whole,
        jax.ShapeDtypeStruct((zs, HALF, key.shape[1]), kind),
        jax.ShapeDtypeStruct((4, 8, 128), jnp.int32),
        jax.ShapeDtypeStruct(tokens.shape, tokens.dtype),
    ]
    one = pltpu.SemaphoreType.DMA
    scratch = [
        pltpu.VMEM((4, 2, zs, HALF, width), kind),
        pltpu.VMEM((2, 2, HALF, width), kind),
        pltpu.VMEM((2, 2, HALF, key.shape[1]), kind),
        pltpu.VMEM((8, 128), jnp.int32),
    ]
    scratch += gather_sems(zs) + [dma(2, zs // 2), dma(2, zs // 2), one, dma(3), dma(3), one]
    body = functools.partial(gather_kernel, zs)
    ins = (owner, counts, first, second, key, value, tokens, gain)
    return call(body, [pltpu.SMEM] * 2 + [pltpu.VMEM] * 6, outs, scratch, 0, "gather_first")(*ins)


def encode_and_sum(piece, normed, tokens, full_in, full_out):
    zs = piece.shape[0]
    spans, _, rows, width = tokens.shape
    kind = tokens.dtype
    whole = jax.ShapeDtypeStruct((width, piece.shape[2]), kind)
    outs = [whole, whole, jax.ShapeDtypeStruct((spans, rows, width), kind)]
    scratch = [
        pltpu.VMEM((4, 2) + piece.shape, kind),
        pltpu.VMEM(tokens.shape, kind),
        pltpu.VMEM((spans, rows, width), jnp.float32),
        pltpu.VMEM((3, spans, rows, width), kind),
        pltpu.VMEM((2, 2, rows, width), kind),
    ]
    scratch += [dma(6), dma(6), dma(3), dma(3), dma(4), dma(4), pltpu.SemaphoreType.DMA]
    body = functools.partial(sums_kernel, zs)
    ins = (piece, normed, tokens, full_in, full_out)
    return call(body, [pltpu.VMEM] * 5, outs, scratch, 1, "encode_and_sum")(*ins)


def route_and_attend(notes, states, key, value, queries):
    spans, rows, width = states.shape
    kind = states.dtype
    outs = [jax.ShapeDtypeStruct(queries.shape, kind)]
    held = pltpu.VMEM((spans, 4, rows, key.shape[1]), kind)
    scratch = [
        pltpu.VMEM((2, rows, width), kind),
        pltpu.VMEM((10, rows, width), kind),
        pltpu.VMEM((spans, 4, rows, width), kind),
        held,
        held,
    ]
    scratch += [dma(3), dma(3), dma(6), dma(6), pltpu.SemaphoreType.DMA]
    ins = [pltpu.SMEM] + [pltpu.VMEM] * 4
    return call(route_kernel, ins, outs, scratch, 2, "route_and_attend")(notes, states, key, value, queries)[0]


def on_device(neighbours, counts, owner, norm_gain, w_in, w_out, w_key, w_value, queries):
    span_count, key_len, enc_width = neighbours.shape
    tokens = neighbours.reshape(span_count, 4, key_len // 4, enc_width)
    full_in, full_out, piece, notes, normed = gather_first(
        owner, counts, w_in, w_out.T, w_key, w_value, tokens, norm_gain
    )
    full_key, full_value, states = encode_and_sum(piece, normed, tokens, full_in, full_out)
    return route_and_attend(notes, states, full_key, full_value, queries)


def solution(mesh):
    placed = (
        P(("grp", "dp"), None, None),
        P(("grp", "dp")),
        P(("grp", "dp")),
        P(),
        P("dp", "mp"),
        P("mp", "dp"),
        P("dp", "mp"),
        P("dp", "mp"),
        P(("grp", "dp"), "mp"),
    )
    return jax.shard_map(
        on_device, mesh=mesh, in_specs=placed, out_specs=P(("grp", "dp"), "mp"), check_vma=False
    )
```
